32 devices in a mesh: tmpl: 4 (over z), chan: 4 (over y, core), tm: 2 (over x).
Axes of the slice: x: 2, y: 2, z: 4, core: 2. Of those that a mesh axis runs over, the one named last changes fastest.
Arguments:
- raw: bfloat16 [256, 4096], P('chan', ('tmpl', 'tm')), may hold values from -6 to 6
- dead_mask: int32 [256], P('chan'), may hold values 0 or 1
- templates: bfloat16 [16, 256, 512], P('tmpl', 'chan'), may hold values from -0.015625 to 0.015625
- assign: int32 [16], P('tmpl'), may hold values from 0 to 15, as said below
- w_enc: bfloat16 [16, 1, 3, 3], replicated, may hold values from -2 to 2
- b_enc: float32 [16], replicated, may hold values from -3 to 3
- w_mid: bfloat16 [32, 16, 3, 3], replicated, may hold values from -0.5 to 0.5
- b_mid: float32 [32], replicated, may hold values from -3 to 3
- w_dec: bfloat16 [16, 48, 3, 3], replicated, may hold values from -0.3125 to 0.3125
- b_dec: float32 [16], replicated, may hold values from -3 to 3
- w_out: bfloat16 [16], replicated, may hold values from -1.5 to 1.5
- b_out: float32 [1], replicated, may hold values from -3 to 3
Outputs:
- denoised: bfloat16 [256, 4096], P('chan', ('tmpl', 'tm'))
- corr: float32 [16, 4, 2, 512], P('tmpl', None, 'tm', 'chan')
The draws below stay inside these ranges and needn't reach their ends.
Inputs may be any that keep to these rules, and one draw needn't show every extreme that they name: `assign`: for each j, entries 4 * j to 4 * j + 3 hold exactly those numbers in some order.
All inputs are finite; a program needn't handle non-finite values. No bound on the sum of `dead_mask` on one device may be relied on, other than what follows from the above.
Results may differ from the reference program's by a relative error of at most 0.018.
Values may be sent and summed in bfloat16 or wider, within the bound.
No kernel may reach another device: no remote copies, remote signals or barrier semaphores. Data moves between devices by JAX's collectives and lax.ppermute only.
A program may use at most 128 MiB of HBM per device.

```python
import math
import jax
import jax.numpy as jnp
from jax import lax

TM_DEV = 4
TL = 512
F = 16
CH = 256
NTMPL = 16
NPAIR = 4
NBLK = 8
NT = 4096


def draw_assign(key, part):
    owners = NTMPL // TM_DEV
    base_ids = jnp.arange(NTMPL, dtype=jnp.int32) // TM_DEV * TM_DEV
    owner_keys = jax.random.split(key, owners)
    orders = jax.vmap(lambda owner_key: jax.random.permutation(owner_key, TM_DEV))(owner_keys)
    return (orders.reshape(-1).astype(jnp.int32) + base_ids).astype(jnp.int32)


def touch_ends(values, own_key, least, largest):
    longest = values.shape.index(max(values.shape))
    spots = []
    for shift in (0, 1):
        where = [jax.random.randint(jax.random.fold_in(own_key, axis), (), 0, length) for axis, length in enumerate(values.shape)]
        where[longest] = (where[longest] + shift) % values.shape[longest]
        spots.append(tuple(where))
    return values.at[spots[0]].set(least).at[spots[1]].set(largest)


def block_scale(own_key, dims, shards, low, largest):
    loudness = 1.0
    for axis_at, shards_of in shards:
        steps = jax.random.uniform(jax.random.fold_in(jax.random.fold_in(own_key, 6), axis_at), (shards_of,), jnp.float32, low / len(shards), largest / len(shards))
        loudness = loudness * jnp.repeat(jnp.exp(steps), dims[axis_at] // shards_of).reshape((-1,) + (1,) * (len(dims) - 1 - axis_at))
    return loudness


def bell_draw(key, dims, spread, reach, cuts=(), kind=jnp.bfloat16):
    level = block_scale(key, dims, cuts, -0.22, 0.18) if cuts else 1.0
    drawn = jax.random.normal(key, dims, jnp.float32) * spread * level
    return jnp.minimum(jnp.maximum(drawn, -reach), reach).astype(kind)


def setup_inputs(seed: int = 0) -> dict:
    streams_of = jax.random.split(jax.random.key(seed), 13)
    return {
        "raw": bell_draw(streams_of[0], (CH, NT), 1.0, 6.0, ((0, 4), (1, 8))),
        "dead_mask": touch_ends((jax.random.randint(streams_of[1], (CH,), 0, 8) < 7).astype(jnp.int32), jax.random.fold_in(streams_of[1], 1), 0, 1),
        "templates": bell_draw(streams_of[2], (NTMPL, CH, TL), (CH * TL) ** -0.5, 0.015625, ((0, 4), (1, 4))),
        "assign": draw_assign(jax.random.fold_in(streams_of[12], 71), 0),
        "w_enc": bell_draw(streams_of[4], (F, 1, 3, 3), 9 ** -0.5, 2.0),
        "b_enc": bell_draw(streams_of[5], (F,), 0.5, 3.0, (), jnp.float32),
        "w_mid": bell_draw(streams_of[6], (2 * F, F, 3, 3), (9 * F) ** -0.5, 0.5),
        "b_mid": bell_draw(streams_of[7], (2 * F,), 0.5, 3.0, (), jnp.float32),
        "w_dec": bell_draw(streams_of[8], (F, 3 * F, 3, 3), (27 * F) ** -0.5, 0.3125),
        "b_dec": bell_draw(streams_of[9], (F,), 0.5, 3.0, (), jnp.float32),
        "w_out": bell_draw(streams_of[10], (F,), F ** -0.5, 1.5),
        "b_out": bell_draw(streams_of[11], (1,), 0.5, 3.0, (), jnp.float32),
    }


def forward_table(patch_len):
    sample_ids = jnp.arange(patch_len, dtype=jnp.int32)[:, None]
    freq_ids = jnp.arange(2 * patch_len, dtype=jnp.int32)[None, :]
    phase = ((sample_ids * freq_ids) % (2 * patch_len)).astype(jnp.float32) * (math.pi / patch_len)
    return jnp.concatenate([jnp.cos(phase), -jnp.sin(phase)], axis=1).astype(jnp.bfloat16)


def inverse_table(patch_len):
    freq_ids = jnp.arange(2 * patch_len, dtype=jnp.int32)[:, None]
    lag_ids = jnp.arange(patch_len, dtype=jnp.int32)[None, :]
    phase = ((freq_ids * lag_ids) % (2 * patch_len)).astype(jnp.float32) * (math.pi / patch_len)
    return jnp.concatenate([jnp.cos(phase), -jnp.sin(phase)], axis=0) / (2.0 * patch_len)


def alternate_signs(patch_len):
    single = jnp.where(jnp.arange(2 * patch_len) % 2 == 0, 1.0, -1.0).astype(jnp.float32)
    return jnp.concatenate([single, single])


def conv_ref(picture, weight, bias_term):
    result = lax.conv_general_dilated(picture.astype(jnp.float32), weight.astype(jnp.float32), (1, 1), ((1, 1), (1, 1)), dimension_numbers=("NCHW", "OIHW", "NCHW"), precision=lax.Precision.HIGHEST)
    return jax.nn.relu(result + bias_term[None, :, None, None]).astype(jnp.bfloat16)


def cross_products(spectrum, tspectrum, half_len):
    spec_re = spectrum[..., :half_len].astype(jnp.float32)
    spec_im = spectrum[..., half_len:].astype(jnp.float32)
    tmpl_re = tspectrum[..., :half_len].astype(jnp.float32)
    tmpl_im = tspectrum[..., half_len:].astype(jnp.float32)
    hp = lax.Precision.HIGHEST
    real_part = jnp.einsum("bcf,kcf->kbf", spec_re, tmpl_re, precision=hp) + jnp.einsum("bcf,kcf->kbf", spec_im, tmpl_im, precision=hp)
    imag_part = jnp.einsum("bcf,kcf->kbf", spec_im, tmpl_re, precision=hp) - jnp.einsum("bcf,kcf->kbf", spec_re, tmpl_im, precision=hp)
    return jnp.concatenate([real_part, imag_part], axis=-1)


def reference(raw, dead_mask, templates, assign, w_enc, b_enc, w_mid, b_mid, w_dec, b_dec, w_out, b_out):
    alive = dead_mask.astype(jnp.float32)
    cleaned = raw * alive[:, None].astype(jnp.bfloat16)
    patches = cleaned.reshape(CH, NBLK, TL).transpose(1, 0, 2)

    def denoise(patch):
        picture = patch[None, None]
        encoded = conv_ref(picture, w_enc, b_enc)
        pooled = encoded.astype(jnp.float32).reshape(1, F, CH // 2, 2, TL // 2, 2).mean(axis=(3, 5)).astype(jnp.bfloat16)
        middle = conv_ref(pooled, w_mid, b_mid)
        upsampled = jnp.repeat(jnp.repeat(middle, 2, axis=2), 2, axis=3)
        merged = jnp.concatenate([upsampled, encoded], axis=1)
        decoded = conv_ref(merged, w_dec, b_dec)
        branch = jnp.einsum("g,gct->ct", w_out.astype(jnp.float32), decoded[0].astype(jnp.float32), precision=lax.Precision.HIGHEST)
        return (alive[:, None] * (patch.astype(jnp.float32) + branch + b_out[0])).astype(jnp.bfloat16)

    denoised_blocks = lax.map(denoise, patches)
    denoised = denoised_blocks.transpose(1, 0, 2).reshape(CH, NT)
    forward = forward_table(TL).astype(jnp.float32)
    spectra = jnp.einsum("bct,tf->bcf", denoised_blocks.astype(jnp.float32), forward, precision=lax.Precision.HIGHEST).astype(jnp.bfloat16)
    tspectra = jnp.einsum("kct,tf->kcf", templates.astype(jnp.float32), forward, precision=lax.Precision.HIGHEST).astype(jnp.bfloat16)
    products = cross_products(spectra, tspectra, 2 * TL)
    following = jnp.concatenate([products[:, 1:], jnp.zeros_like(products[:, :1])], axis=1)
    combined = products + alternate_signs(TL) * following
    lagged = jnp.dot(combined.reshape(-1, 4 * TL), inverse_table(TL), precision=lax.Precision.HIGHEST).reshape(NTMPL, NBLK, TL)
    ordered = lagged[assign]
    return denoised, ordered.reshape(NTMPL, NPAIR, 2, TL)
```

```python
import functools
import math

import jax
import jax.numpy as jnp
import numpy as np
from jax import lax
from jax.experimental import pallas as pl
from jax.experimental.pallas import tpu as pltpu
from jax.sharding import PartitionSpec as P

BF = jnp.bfloat16
F32 = jnp.float32
EDGE = 8
ENC_ROWS = 8
MID_ROWS = 7
DEC_ROWS = 8
OFF = -1e30


def frequency_order(patch_len):
    return np.concatenate([np.arange(0, patch_len, 2), np.arange(1, patch_len, 2)])


def forward_table(patch_len):
    s = np.arange(patch_len)[:, None]
    f = frequency_order(patch_len)[None, :]
    phase = ((s * f) % (2 * patch_len)).astype(np.float64) * (math.pi / patch_len)
    table = np.concatenate([np.cos(phase), np.sin(phase)], axis=1)
    table[:, patch_len] = 1.0 - 2.0 * (np.arange(patch_len) % 2)
    return table.astype(jnp.bfloat16)


def inverse_table(patch_len):
    table = forward_table(patch_len).astype(np.float32).T.copy()
    table[0] *= 0.5
    table[patch_len] *= 0.5
    return table.astype(jnp.bfloat16)


def dot(a, b):
    return jnp.dot(a, b, preferred_element_type=F32)


def iota(shape, dim):
    return lax.broadcasted_iota(jnp.int32, shape, dim)


def column(row, count):
    m = row.shape[1]
    pick = iota((count, m), 0) % m == iota((count, m), 1)
    return jnp.sum(jnp.where(pick, row, 0.0), axis=1, keepdims=True)


def prep_kernel(
    we_ref, wm_ref, ws_ref, wu_ref, be_ref, bm_ref, bd_ref, wo_ref,
    enc_ref, mid_ref, dec_ref, out_ref, benc_ref, bmid_ref, bdec_ref, wide_ref,
):
    maps = we_ref.shape[0]
    half = benc_ref.shape[1]
    rows, cols = enc_ref.shape
    window = ENC_ROWS + EDGE
    spread = jnp.where(iota((rows, maps), 0) % maps == iota((rows, maps), 1), 1.0, 0.0).astype(BF)
    taps = dot(spread, we_ref[...])
    row_id = iota((rows, cols), 0)
    col_id = iota((rows, cols), 1)
    dy = col_id % window - row_id // (4 * maps) - (EDGE // 2 - 1)
    dx = col_id // window - row_id // maps % 4
    tap = jnp.where((dy >= 0) & (dy < 3) & (dx >= 0) & (dx < 3), dy * 3 + dx, -1)
    acc = jnp.zeros((rows, cols), F32)
    for t in range(9):
        acc = jnp.where(tap == t, taps[:, t : t + 1], acc)
    enc_ref[...] = acc.astype(BF)
    wide_ref[...] = jnp.zeros(wide_ref.shape, F32)
    wm = wm_ref[...].astype(F32)
    for r in range(MID_ROWS):
        wide_ref[r * 2 * maps : (r + 1) * 2 * maps, r * 3 * maps : r * 3 * maps + 9 * maps] = wm
    mid_ref[...] = wide_ref[: mid_ref.shape[0], : mid_ref.shape[1]].astype(BF)
    wide_ref[...] = jnp.zeros(wide_ref.shape, F32)
    ws = ws_ref[...].astype(F32)
    wu = wu_ref[...].astype(F32)
    skip_cols = (DEC_ROWS + 2) * 4 * maps
    k = [[wu[:, (y * 3 + x) * 2 * maps : (y * 3 + x + 1) * 2 * maps] for x in range(3)] for y in range(3)]
    for r in range(DEC_ROWS):
        ys = ((0,), (1, 2)) if r % 2 == 0 else ((0, 1), (2,))
        for q in range(2):
            top = (r * 2 + q) * maps
            for y in range(3):
                left = ((r + y) * 4 + q) * maps
                wide_ref[top : top + maps, left : left + 3 * maps] = ws[:, y * 3 * maps : (y + 1) * 3 * maps]
            xs = ((0,), (1, 2)) if q == 0 else ((0, 1), (2,))
            for a in range(2):
                for b in range(2):
                    value = sum(k[y][x] for y in ys[a] for x in xs[b])
                    left = skip_cols + ((r + 1) // 2 + a) * 6 * maps + (q + b) * 2 * maps
                    wide_ref[top : top + maps, left : left + 2 * maps] = value
    dec_ref[...] = wide_ref[...].astype(BF)
    n = out_ref.shape[1]
    repeat = jnp.where(iota((maps, n), 1) % maps == iota((maps, n), 0), 1.0, 0.0).astype(BF)
    weights = dot(wo_ref[...], repeat)
    r_id = iota(out_ref.shape, 0)
    c_id = iota(out_ref.shape, 1)
    same = (c_id // (2 * maps) == r_id % DEC_ROWS) & (c_id // maps % 2 == r_id // DEC_ROWS)
    out_ref[...] = jnp.where(same, weights, 0.0).astype(BF)
    lane = iota((4 * maps, half), 1)
    q = iota((4 * maps, half), 0) // maps
    outside = ((q == 0) & (lane == 0)) | ((q == 3) & (lane == half - 1))
    benc_ref[...] = jnp.where(outside, OFF, column(be_ref[...], 4 * maps))
    bmid_ref[...] = jnp.broadcast_to(column(bm_ref[...], 2 * maps), bmid_ref.shape)
    bdec_ref[...] = jnp.broadcast_to(column(bd_ref[...], 2 * maps), bdec_ref.shape)


def shifted(x, by):
    width = x.shape[1]
    lane = iota(x.shape, 1)
    edge = 0 if by < 0 else width - 1
    return jnp.where(lane == edge, 0.0, pltpu.roll(x, (-by) % width, 1))


def unet_kernel(
    raw_ref, mask_ref, r1_ref, r2_ref, enc_ref, mid_ref, dec_ref, wout_ref, benc_ref, bmid_ref, bdec_ref, bout_ref,
    out_ref, xs_ref, e4_ref, p3_ref, m3_ref, de_ref, do_ref,
):
    rows, length = raw_ref.shape
    half = length // 2
    maps = benc_ref.shape[0] // 4
    here = lax.axis_index("chan")
    last = lax.axis_size("chan") - 1
    odd = here % 2 == 1
    keep_top = jnp.where(here == 0, 0.0, 1.0)
    keep_bottom = jnp.where(here == last, 0.0, 1.0)
    alive = column(mask_ref[...].astype(F32), rows)
    r1 = r1_ref[...].astype(F32)
    r2 = r2_ref[...].astype(F32)
    cleaned = raw_ref[...].astype(F32) * alive
    x = jnp.concatenate([jnp.where(odd, r1, r2), cleaned, jnp.where(odd, r2, r1)], axis=0).astype(BF)
    s = iota((length, half), 0)
    t = iota((length, half), 1)
    even = dot(x, jnp.where(s == 2 * t, 1.0, 0.0).astype(BF))
    uneven = dot(x, jnp.where(s == 2 * t + 1, 1.0, 0.0).astype(BF))
    for d, piece in enumerate((shifted(even, -1), shifted(uneven, -1), even, uneven, shifted(even, 1), shifted(uneven, 1))):
        xs_ref[d] = piece
    span = 4 * maps
    groups = (rows + EDGE) // ENC_ROWS
    margin = EDGE // 2
    p3_ref[...] = jnp.zeros(p3_ref.shape, BF)
    for g in range(groups):
        start = g * ENC_ROWS
        window = jnp.concatenate([xs_ref[d, start : start + ENC_ROWS + EDGE, :] for d in range(6)], axis=0).astype(BF)
        y = dot(enc_ref[...], window).reshape(ENC_ROWS, span, half)
        y = jnp.maximum(y + benc_ref[...][None], 0.0)
        pieces = []
        for r in range(ENC_ROWS):
            row = start + r - margin
            piece = y[r]
            if row < 0:
                piece = piece * keep_top
            if row >= rows:
                piece = piece * keep_bottom
            piece = piece.astype(BF)
            e4_ref[(start + r) * span : (start + r + 1) * span, :] = piece
            pieces.append(piece[maps : 3 * maps].astype(F32))
        for r in range(0, ENC_ROWS, 2):
            both = pieces[r] + pieces[r + 1]
            pooled = ((both[:maps] + both[maps:]) * 0.25).astype(BF).astype(F32)
            at = (start + r) // 2 * 3 * maps
            p3_ref[at : at + 3 * maps, :] = jnp.concatenate([shifted(pooled, -1), pooled, shifted(pooled, 1)], axis=0).astype(BF)
    span_p = 3 * maps
    span_m = 6 * maps
    mid_total = rows // 2 + 2
    for g in range(-(-mid_total // MID_ROWS)):
        start = g * MID_ROWS
        y = dot(mid_ref[...], p3_ref[start * span_p : (start + MID_ROWS + 2) * span_p, :]).reshape(MID_ROWS, 2 * maps, half)
        y = jnp.maximum(y + bmid_ref[...][None], 0.0)
        for r in range(MID_ROWS):
            row = start + r - 1
            if row > rows // 2:
                continue
            piece = y[r]
            if row < 0:
                piece = piece * keep_top
            if row >= rows // 2:
                piece = piece * keep_bottom
            piece = piece.astype(BF).astype(F32)
            m3_ref[(start + r) * span_m : (start + r + 1) * span_m, :] = jnp.concatenate(
                [shifted(piece, -1), piece, shifted(piece, 1)], axis=0
            ).astype(BF)
    for g in range(rows // DEC_ROWS):
        start = g * DEC_ROWS
        skip = e4_ref[(start + margin - 1) * span : (start + margin + DEC_ROWS + 1) * span, :]
        up = m3_ref[start // 2 * span_m : (start // 2 + DEC_ROWS // 2 + 2) * span_m, :]
        y = dot(dec_ref[...], jnp.concatenate([skip, up], axis=0)).reshape(DEC_ROWS, 2 * maps, half)
        y = jnp.maximum(y + bdec_ref[...][None], 0.0).astype(BF).reshape(DEC_ROWS * 2 * maps, half)
        branch = dot(wout_ref[...], y)
        live = alive[start : start + DEC_ROWS]
        at = start + EDGE
        for q, ref in ((0, de_ref), (1, do_ref)):
            own = xs_ref[2 + q, at : at + DEC_ROWS, :]
            ref[start : start + DEC_ROWS, :] = live * (own + branch[q * DEC_ROWS : (q + 1) * DEC_ROWS] + bout_ref[0])
    s = iota((half, length), 1)
    t = iota((half, length), 0)
    out_ref[...] = (
        dot(de_ref[...].astype(BF), jnp.where(s == 2 * t, 1.0, 0.0).astype(BF))
        + dot(do_ref[...].astype(BF), jnp.where(s == 2 * t + 1, 1.0, 0.0).astype(BF))
    ).astype(BF)


def template_kernel(t_ref, table_ref, a_ref, b_ref, first_ref):
    count, rows, length = t_ref.shape
    for k in range(count):
        y = dot(t_ref[k], table_ref[...]).astype(BF).astype(F32)
        a = y[:, :length]
        b = y[:, length:]
        lane = iota(a.shape, 1)
        a_ref[k] = a
        b_ref[k] = jnp.where(lane == 0, 0.0, b)
        first_ref[k] = jnp.where(lane == 0, b, a)[:, :128]


def corr_kernel(count, *refs):
    x_refs = refs[:count]
    ta_ref, tb_ref, tf_ref, table_ref, inverse_ref, assign_ref = refs[count : count + 6]
    outs = refs[count + 6 : -3]
    sa_ref, p_ref, share_ref = refs[-3:]
    rows, length = x_refs[0].shape
    tmpl = ta_ref.shape[0]
    here = lax.axis_index("tmpl")
    for k in range(count):
        sa_ref[(here - k) % count] = dot(x_refs[k][...], table_ref[...]).astype(BF).astype(F32)
    picks = [assign_ref[r] % tmpl for r in range(tmpl)]
    for lane in range(0, length, 128):
        real = [[None] * count for _ in range(tmpl)]
        imag = [[None] * count for _ in range(tmpl)]
        for c in range(0, rows, 8):
            at = [ta_ref[picks[r], c : c + 8, lane : lane + 128] for r in range(tmpl)]
            bt = [tb_ref[picks[r], c : c + 8, lane : lane + 128] for r in range(tmpl)]
            af = at if lane else [tf_ref[picks[r], c : c + 8, :] for r in range(tmpl)]
            for i in range(count):
                ax = sa_ref[i, c : c + 8, lane : lane + 128]
                bx = sa_ref[i, c : c + 8, length + lane : length + lane + 128]
                for r in range(tmpl):
                    re = ax * at[r] + bx * bt[r]
                    im = bx * af[r] - ax * bt[r]
                    real[r][i] = re if c == 0 else real[r][i] + re
                    imag[r][i] = im if c == 0 else imag[r][i] + im
        for r in range(tmpl):
            for i in range(count):
                row = r * count + i
                p_ref[row : row + 1, lane : lane + 128] = jnp.sum(real[r][i], axis=0, keepdims=True)
                p_ref[row : row + 1, length + lane : length + lane + 128] = jnp.sum(imag[r][i], axis=0, keepdims=True)
    p = p_ref[...]
    high = p.astype(BF)
    low = (p - high.astype(F32)).astype(BF)
    pairs = tmpl * count
    both = jnp.concatenate([high, low], axis=0)
    half = length // 2

    def part(first):
        y = dot(both[:, first : first + half], inverse_ref[first : first + half, :]) + dot(
            both[:, length + first : length + first + half], inverse_ref[length + first : length + first + half, :]
        )
        return (y[:pairs] + y[pairs:]) * (1.0 / length)

    even = part(0)
    uneven = part(half)
    near = even + uneven
    far = even - uneven
    block = iota(far.shape, 0) % count
    later = jnp.where(block == count - 1, 0.0, pltpu.roll(far, pairs - 1, 0))
    parity = lax.axis_index("tm")
    far = jnp.where(parity == 1, far, later)
    width = share_ref.shape[3]
    chans = share_ref.shape[1]
    for c in range(chans):
        share_ref[0, c] = near[:, c * width : (c + 1) * width]
        share_ref[1, c] = far[:, c * width : (c + 1) * width]
    chan = lax.axis_index("chan")
    for k, out in enumerate(outs):
        to = (chan * 2 + parity + k) % (2 * chans)
        out[...] = share_ref[(to + parity) % 2, to // 2].astype(BF)


def call(kernel, outs, scratch=(), smem=(), inputs=0, name=None):
    return pl.pallas_call(
        kernel,
        out_shape=tuple(jax.ShapeDtypeStruct(s, d) for s, d in outs),
        in_specs=[
            pl.BlockSpec(memory_space=pltpu.SMEM if i in smem else pltpu.VMEM) for i in range(inputs)
        ],
        out_specs=tuple(pl.BlockSpec(memory_space=pltpu.VMEM) for _ in outs),
        scratch_shapes=scratch,
        name=name,
        compiler_params=pltpu.CompilerParams(vmem_limit_bytes=48 * 1024 * 1024),
    )


def rotated(x, axes, by):
    count = lax.axis_size(axes)
    return lax.ppermute(x, axes, [(i, (i + by) % count) for i in range(count)])


def body(raw, dead_mask, templates, assign, w_enc, b_enc, w_mid, b_mid, w_dec, b_dec, w_out, b_out):
    rows, length = raw.shape
    half = length // 2
    maps = w_enc.shape[0]
    chans = lax.axis_size("chan")
    blocks = lax.axis_size("tmpl")
    tmpl = templates.shape[0]
    odd = lax.axis_index("chan") % 2 == 1
    alive = dead_mask.astype(BF)[:, None]
    head = raw[:EDGE] * alive[:EDGE]
    tail = raw[-EDGE:] * alive[-EDGE:]
    r1 = lax.ppermute(jnp.where(odd, head, tail), "chan", [(i, i ^ 1) for i in range(chans) if i ^ 1 < chans])
    links = [(i, i + 1) for i in range(1, chans - 1, 2)]
    r2 = lax.ppermute(jnp.where(odd, tail, head), "chan", links + [(b, a) for a, b in links])

    dec_cols = (DEC_ROWS + 2) * 4 * maps + (DEC_ROWS // 2 + 2) * 6 * maps
    weights = call(
        prep_kernel,
        [
            ((ENC_ROWS * 4 * maps, 6 * (ENC_ROWS + EDGE)), BF),
            ((MID_ROWS * 2 * maps, (MID_ROWS + 2) * 3 * maps), BF),
            ((DEC_ROWS * 2 * maps, dec_cols), BF),
            ((2 * DEC_ROWS, DEC_ROWS * 2 * maps), BF),
            ((4 * maps, half), F32),
            ((2 * maps, half), F32),
            ((2 * maps, half), F32),
        ],
        [pltpu.VMEM((DEC_ROWS * 2 * maps, dec_cols), F32)],
        inputs=8,
        name="prep",
    )(
        w_enc.reshape(maps, 9),
        w_mid.transpose(0, 2, 3, 1).reshape(2 * maps, 9 * maps),
        w_dec[:, 2 * maps :].transpose(0, 2, 3, 1).reshape(maps, 9 * maps),
        w_dec[:, : 2 * maps].transpose(0, 2, 3, 1).reshape(maps, 18 * maps),
        b_enc[None],
        b_mid[None],
        b_dec[None],
        w_out[None],
    )
    mid_groups = -(-(rows // 2 + 2) // MID_ROWS)
    (denoised,) = call(
        unet_kernel,
        [((rows, length), BF)],
        [
            pltpu.VMEM((6, rows + 2 * EDGE, half), F32),
            pltpu.VMEM(((rows + EDGE) * 4 * maps, half), BF),
            pltpu.VMEM(((mid_groups * MID_ROWS + 2) * 3 * maps, half), BF),
            pltpu.VMEM(((rows // 2 + 2) * 6 * maps, half), BF),
            pltpu.VMEM((rows, half), F32),
            pltpu.VMEM((rows, half), F32),
        ],
        smem=(11,),
        inputs=12,
        name="unet",
    )(raw, dead_mask[None], r1, r2, *weights, b_out)

    forward = jnp.asarray(forward_table(length))
    inverse = jnp.asarray(inverse_table(length))
    spectra_t = call(
        template_kernel,
        [((tmpl, rows, length), F32), ((tmpl, rows, length), F32), ((tmpl, rows, 128), F32)],
        inputs=2,
        name="tspectra",
    )(templates, forward)
    gathered = [denoised] + [rotated(denoised, "tmpl", k) for k in range(1, blocks)]
    width = length // chans
    pairs = tmpl * blocks
    sent = call(
        functools.partial(corr_kernel, blocks),
        [((pairs, width), BF)] * (2 * chans),
        [
            pltpu.VMEM((blocks, rows, 2 * length), F32),
            pltpu.VMEM((pairs, 2 * length), F32),
            pltpu.VMEM((2, chans, pairs, width), F32),
        ],
        smem=(blocks + 5,),
        inputs=blocks + 6,
        name="corr",
    )(*gathered, *spectra_t, forward, inverse, assign)
    total = sent[0].astype(F32)
    for k in range(1, 2 * chans):
        total = total + rotated(sent[k], ("chan", "tm"), k).astype(F32)
    return denoised, total.reshape(tmpl, blocks, 1, width)


def solution(mesh):
    return jax.shard_map(
        body,
        mesh=mesh,
        in_specs=(
            P("chan", ("tmpl", "tm")),
            P("chan"),
            P("tmpl", "chan", None),
            P("tmpl"),
            P(),
            P(),
            P(),
            P(),
            P(),
            P(),
            P(),
            P(),
        ),
        out_specs=(P("chan", ("tmpl", "tm")), P("tmpl", None, "tm", "chan")),
        check_vma=False,
    )
```

```python
import functools
import math

import jax
import jax.numpy as jnp
import numpy as np
from jax import lax
from jax.experimental import pallas as pl
from jax.experimental.pallas import tpu as pltpu
from jax.sharding import PartitionSpec as P

BF = jnp.bfloat16
F32 = jnp.float32
EDGE = 8
ENC_ROWS = 8
MID_ROWS = 7
DEC_ROWS = 8
OFF = -1e30


def frequency_order(patch_len):
    return np.concatenate([np.arange(0, patch_len, 2), np.arange(1, patch_len, 2)])


def forward_table(patch_len):
    s = np.arange(patch_len)[:, None]
    f = frequency_order(patch_len)[None, :]
    phase = ((s * f) % (2 * patch_len)).astype(np.float64) * (math.pi / patch_len)
    table = np.concatenate([np.cos(phase), np.sin(phase)], axis=1)
    table[:, patch_len] = 1.0 - 2.0 * (np.arange(patch_len) % 2)
    return table.astype(jnp.bfloat16)


def inverse_table(patch_len):
    table = forward_table(patch_len).astype(np.float32).T.copy()
    table[0] *= 0.5
    table[patch_len] *= 0.5
    return table.astype(jnp.bfloat16)


def dot(a, b):
    return jnp.dot(a, b, preferred_element_type=F32)


def iota(shape, dim):
    return lax.broadcasted_iota(jnp.int32, shape, dim)


def column(row, count):
    m = row.shape[1]
    pick = iota((count, m), 0) % m == iota((count, m), 1)
    return jnp.sum(jnp.where(pick, row, 0.0), axis=1, keepdims=True)


def load_kernel(*refs):
    count = (len(refs) - 3) // 2
    sources = refs[:count]
    copies = refs[count : 2 * count]
    first_ref, second_ref, sems = refs[2 * count :]
    moves = [pltpu.make_async_copy(src, dst, sems.at[i]) for i, (src, dst) in enumerate(zip(sources, copies))]
    for move in moves:
        move.start()
    moves[0].wait()
    moves[1].wait()
    raw_ref, mask_ref = copies[:2]
    rows = raw_ref.shape[0]
    alive = column(mask_ref[...].astype(F32), rows)
    head = raw_ref[:EDGE].astype(F32) * alive[:EDGE]
    tail = raw_ref[rows - EDGE :].astype(F32) * alive[rows - EDGE :]
    odd = lax.axis_index("chan") % 2 == 1
    first_ref[...] = jnp.where(odd, head, tail).astype(BF)
    second_ref[...] = jnp.where(odd, tail, head).astype(BF)
    for move in moves[2:]:
        move.wait()


def prep_kernel(
    we_ref, wm_ref, wd_ref, be_ref, bm_ref, bd_ref, wo_ref,
    enc_ref, mid_ref, dec_ref, out_ref, benc_ref, bmid_ref, bdec_ref, wide_ref,
):
    maps = we_ref.shape[3]
    half = benc_ref.shape[1]
    rows, cols = enc_ref.shape
    window = ENC_ROWS + EDGE
    spread = jnp.where(iota((rows, maps), 0) % maps == iota((rows, maps), 1), 1.0, 0.0).astype(BF)
    we = jnp.concatenate([we_ref[0, y].astype(F32) for y in range(3)], axis=0).astype(BF)
    taps = lax.dot_general(spread, we, (((1,), (1,)), ((), ())), preferred_element_type=F32)
    row_id = iota((rows, cols), 0)
    col_id = iota((rows, cols), 1)
    dy = col_id % window - row_id // (4 * maps) - (EDGE // 2 - 1)
    dx = col_id // window - row_id // maps % 4
    tap = jnp.where((dy >= 0) & (dy < 3) & (dx >= 0) & (dx < 3), dy * 3 + dx, -1)
    acc = jnp.zeros((rows, cols), F32)
    for t in range(9):
        acc = jnp.where(tap == t, taps[:, t : t + 1], acc)
    enc_ref[...] = acc.astype(BF)
    wide_ref[...] = jnp.zeros(wide_ref.shape, F32)
    wm = wm_ref[...].astype(F32).reshape(9 * maps, 2 * maps).T
    for r in range(MID_ROWS):
        wide_ref[r * 2 * maps : (r + 1) * 2 * maps, r * 3 * maps : r * 3 * maps + 9 * maps] = wm
    mid_ref[...] = wide_ref[: mid_ref.shape[0], : mid_ref.shape[1]].astype(BF)
    wide_ref[...] = jnp.zeros(wide_ref.shape, F32)
    skip_cols = (DEC_ROWS + 2) * 4 * maps
    k = [[wd_ref[y, x].astype(F32) for x in range(3)] for y in range(3)]
    ws = [jnp.concatenate([k[y][x][:, 2 * maps :] for x in range(3)], axis=1) for y in range(3)]
    split = ((0,), (1, 2)), ((0, 1), (2,))
    wu = {}
    for r in range(2):
        for q in range(2):
            for a in range(2):
                wu[r, q, a] = jnp.concatenate(
                    [sum(k[y][x][:, : 2 * maps] for y in split[r][a] for x in split[q][b]) for b in range(2)], axis=1
                )
    for r in range(DEC_ROWS):
        for q in range(2):
            top = (r * 2 + q) * maps
            for y in range(3):
                left = ((r + y) * 4 + q) * maps
                wide_ref[top : top + maps, left : left + 3 * maps] = ws[y]
            for a in range(2):
                left = skip_cols + ((r + 1) // 2 + a) * 6 * maps + q * 2 * maps
                wide_ref[top : top + maps, left : left + 4 * maps] = wu[r % 2, q, a]
    dec_ref[...] = wide_ref[...].astype(BF)
    n = out_ref.shape[1]
    repeat = jnp.where(iota((maps, n), 1) % maps == iota((maps, n), 0), 1.0, 0.0).astype(BF)
    weights = dot(wo_ref[...], repeat)
    r_id = iota(out_ref.shape, 0)
    c_id = iota(out_ref.shape, 1)
    same = (c_id // (2 * maps) == r_id % DEC_ROWS) & (c_id // maps % 2 == r_id // DEC_ROWS)
    out_ref[...] = jnp.where(same, weights, 0.0).astype(BF)
    lane = iota((4 * maps, half), 1)
    q = iota((4 * maps, half), 0) // maps
    outside = ((q == 0) & (lane == 0)) | ((q == 3) & (lane == half - 1))
    benc_ref[...] = jnp.where(outside, OFF, column(be_ref[...], 4 * maps))
    bmid_ref[...] = jnp.broadcast_to(column(bm_ref[...], 2 * maps), bmid_ref.shape)
    bdec_ref[...] = jnp.broadcast_to(column(bd_ref[...], 2 * maps), bdec_ref.shape)


def shifted(x, by):
    width = x.shape[1]
    lane = iota(x.shape, 1)
    edge = 0 if by < 0 else width - 1
    return jnp.where(lane == edge, 0.0, pltpu.roll(x, (-by) % width, 1))


def unet_kernel(
    raw_ref, mask_ref, r1_ref, r2_ref, enc_ref, mid_ref, dec_ref, wout_ref, benc_ref, bmid_ref, bdec_ref, bout_ref,
    out_ref, xs_ref, e4_ref, p3_ref, m3_ref, de_ref, do_ref,
):
    rows, length = raw_ref.shape
    half = length // 2
    maps = benc_ref.shape[0] // 4
    here = lax.axis_index("chan")
    last = lax.axis_size("chan") - 1
    odd = here % 2 == 1
    keep_top = jnp.where(here == 0, 0.0, 1.0)
    keep_bottom = jnp.where(here == last, 0.0, 1.0)
    alive = column(mask_ref[...].astype(F32), rows)
    r1 = r1_ref[...].astype(F32)
    r2 = r2_ref[...].astype(F32)
    cleaned = raw_ref[...].astype(F32) * alive
    x = jnp.concatenate([jnp.where(odd, r1, r2), cleaned, jnp.where(odd, r2, r1)], axis=0).astype(BF)
    s = iota((length, half), 0)
    t = iota((length, half), 1)
    even = dot(x, jnp.where(s == 2 * t, 1.0, 0.0).astype(BF))
    uneven = dot(x, jnp.where(s == 2 * t + 1, 1.0, 0.0).astype(BF))
    for d, piece in enumerate((shifted(even, -1), shifted(uneven, -1), even, uneven, shifted(even, 1), shifted(uneven, 1))):
        xs_ref[d] = piece
    span = 4 * maps
    groups = (rows + EDGE) // ENC_ROWS
    margin = EDGE // 2
    p3_ref[...] = jnp.zeros(p3_ref.shape, BF)
    for g in range(groups):
        start = g * ENC_ROWS
        window = jnp.concatenate([xs_ref[d, start : start + ENC_ROWS + EDGE, :] for d in range(6)], axis=0).astype(BF)
        y = dot(enc_ref[...], window).reshape(ENC_ROWS, span, half)
        y = jnp.maximum(y + benc_ref[...][None], 0.0)
        pieces = []
        for r in range(ENC_ROWS):
            row = start + r - margin
            piece = y[r]
            if row < 0:
                piece = piece * keep_top
            if row >= rows:
                piece = piece * keep_bottom
            piece = piece.astype(BF)
            e4_ref[(start + r) * span : (start + r + 1) * span, :] = piece
            pieces.append(piece[maps : 3 * maps].astype(F32))
        for r in range(0, ENC_ROWS, 2):
            both = pieces[r] + pieces[r + 1]
            pooled = ((both[:maps] + both[maps:]) * 0.25).astype(BF).astype(F32)
            at = (start + r) // 2 * 3 * maps
            p3_ref[at : at + 3 * maps, :] = jnp.concatenate([shifted(pooled, -1), pooled, shifted(pooled, 1)], axis=0).astype(BF)
    span_p = 3 * maps
    span_m = 6 * maps
    mid_total = rows // 2 + 2
    for g in range(-(-mid_total // MID_ROWS)):
        start = g * MID_ROWS
        y = dot(mid_ref[...], p3_ref[start * span_p : (start + MID_ROWS + 2) * span_p, :]).reshape(MID_ROWS, 2 * maps, half)
        y = jnp.maximum(y + bmid_ref[...][None], 0.0)
        for r in range(MID_ROWS):
            row = start + r - 1
            if row > rows // 2:
                continue
            piece = y[r]
            if row < 0:
                piece = piece * keep_top
            if row >= rows // 2:
                piece = piece * keep_bottom
            piece = piece.astype(BF).astype(F32)
            m3_ref[(start + r) * span_m : (start + r + 1) * span_m, :] = jnp.concatenate(
                [shifted(piece, -1), piece, shifted(piece, 1)], axis=0
            ).astype(BF)
    for g in range(rows // DEC_ROWS):
        start = g * DEC_ROWS
        skip = e4_ref[(start + margin - 1) * span : (start + margin + DEC_ROWS + 1) * span, :]
        up = m3_ref[start // 2 * span_m : (start // 2 + DEC_ROWS // 2 + 2) * span_m, :]
        y = dot(dec_ref[...], jnp.concatenate([skip, up], axis=0)).reshape(DEC_ROWS, 2 * maps, half)
        y = jnp.maximum(y + bdec_ref[...][None], 0.0).astype(BF).reshape(DEC_ROWS * 2 * maps, half)
        branch = dot(wout_ref[...], y)
        live = alive[start : start + DEC_ROWS]
        at = start + EDGE
        for q, ref in ((0, de_ref), (1, do_ref)):
            own = xs_ref[2 + q, at : at + DEC_ROWS, :]
            ref[start : start + DEC_ROWS, :] = live * (own + branch[q * DEC_ROWS : (q + 1) * DEC_ROWS] + bout_ref[0])
    s = iota((half, length), 1)
    t = iota((half, length), 0)
    out_ref[...] = (
        dot(de_ref[...].astype(BF), jnp.where(s == 2 * t, 1.0, 0.0).astype(BF))
        + dot(do_ref[...].astype(BF), jnp.where(s == 2 * t + 1, 1.0, 0.0).astype(BF))
    ).astype(BF)


def products(spectra, ta_ref, tb_ref, tf_ref, put):
    tmpl, rows, length = ta_ref.shape
    count = len(spectra)
    for lane in range(0, length, 128):
        real = {}
        imag = {}
        for c in range(0, rows, 8):
            at = [ta_ref[r, c : c + 8, lane : lane + 128] for r in range(tmpl)]
            bt = [tb_ref[r, c : c + 8, lane : lane + 128] for r in range(tmpl)]
            af = at if lane else [tf_ref[r, c : c + 8, :] for r in range(tmpl)]
            for i in range(count):
                ax = spectra[i][c : c + 8, lane : lane + 128]
                bx = spectra[i][c : c + 8, length + lane : length + lane + 128]
                for r in range(tmpl):
                    re = ax * at[r] + bx * bt[r]
                    im = bx * af[r] - ax * bt[r]
                    real[r, i] = re if c == 0 else real[r, i] + re
                    imag[r, i] = im if c == 0 else imag[r, i] + im
        for r in range(tmpl):
            for i in range(count):
                put(r, i, lane, jnp.sum(real[r, i], axis=0, keepdims=True))
                put(r, i, length + lane, jnp.sum(imag[r, i], axis=0, keepdims=True))


def own_kernel(x_ref, t_ref, table_ref, assign_ref, a_ref, b_ref, first_ref, p_ref, order_ref, s_ref, sem):
    fetch = pltpu.make_async_copy(assign_ref, order_ref, sem)
    fetch.start()
    tmpl, rows, length = t_ref.shape
    s_ref[...] = dot(x_ref[...], table_ref[...])
    fetch.wait()
    for r in range(tmpl):
        y = dot(t_ref[order_ref[r] % tmpl], table_ref[...])
        a = y[:, :length]
        b = y[:, length:]
        lane = iota((rows, 128), 1)
        a_ref[r] = a
        b_ref[r] = b
        b_ref[r, :, :128] = jnp.where(lane == 0, 0.0, b[:, :128])
        first_ref[r] = jnp.where(lane == 0, b[:, :128], a[:, :128])

    def put(r, i, lane, row):
        p_ref[r : r + 1, lane : lane + 128] = row

    products([s_ref], a_ref, b_ref, first_ref, put)


def corr_kernel(others, *refs):
    x_refs = refs[: others + 1]
    ta_ref, tb_ref, tf_ref, own_ref, table_ref, inverse_ref = refs[others + 1 : others + 7]
    copy_ref, keep_ref, send_ref, s_ref, p_ref, share_ref, sem = refs[others + 7 :]
    store = pltpu.make_async_copy(x_refs[0], copy_ref, sem)
    store.start()
    count = others + 1
    tmpl, rows, length = ta_ref.shape
    here = lax.axis_index("tmpl")
    p_ref[here] = own_ref[...]
    if others:
        s_ref[...] = dot(jnp.concatenate([x_ref[...] for x_ref in x_refs[1:]], axis=0), table_ref[...])

    def put(r, i, lane, row):
        p_ref[(here + others - i) % count, r : r + 1, lane : lane + 128] = row

    products([s_ref.at[i * rows : (i + 1) * rows] for i in range(others)], ta_ref, tb_ref, tf_ref, put)
    p = jnp.concatenate([p_ref[i, r : r + 1, :] for r in range(tmpl) for i in range(count)], axis=0)
    high = p.astype(BF)
    low = (p - high.astype(F32)).astype(BF)
    pairs = tmpl * count
    both = jnp.concatenate([high, low], axis=0)
    half = length // 2

    def part(first):
        y = dot(both[:, first : first + half], inverse_ref[first : first + half, :]) + dot(
            both[:, length + first : length + first + half], inverse_ref[length + first : length + first + half, :]
        )
        return (y[:pairs] + y[pairs:]) * (1.0 / length)

    even = part(0)
    uneven = part(half)
    near = even + uneven
    far = even - uneven
    block = iota(far.shape, 0) % count
    later = jnp.where(block == count - 1, 0.0, pltpu.roll(far, pairs - 1, 0))
    parity = lax.axis_index("tm")
    far = jnp.where(parity == 1, far, later)
    width = share_ref.shape[3]
    chans = share_ref.shape[1]
    for c in range(chans):
        share_ref[0, c] = near[:, c * width : (c + 1) * width]
        share_ref[1, c] = far[:, c * width : (c + 1) * width]
    chan = lax.axis_index("chan")
    mine = chan // 2 * 2 + parity
    for k in range(chans):
        to = mine ^ k
        kind = (to + parity) % 2
        keep_ref[k] = share_ref[kind, to // 2 * 2 + chan % 2]
        send_ref[k] = share_ref[kind, to // 2 * 2 + 1 - chan % 2].astype(BF)
    store.wait()


def fold_kernel(keep_ref, got_ref, own_ref, *outs):
    own_ref[...] = keep_ref[0] + got_ref[0].astype(F32)
    for k, out in enumerate(outs):
        out[...] = (keep_ref[k + 1] + got_ref[k + 1].astype(F32)).astype(BF)


VMEM = pltpu.MemorySpace.VMEM
HBM = pltpu.MemorySpace.HBM
SMEM = pltpu.MemorySpace.SMEM


def call(kernel, outs, scratch=(), hbm=(), smem=(), hbm_out=(), inputs=0, name=None):
    def run(*args):
        return inner(*[pltpu.with_memory_space_constraint(x, HBM) if i in hbm else x for i, x in enumerate(args)])

    inner = pl.pallas_call(
        kernel,
        out_shape=tuple(jax.ShapeDtypeStruct(s, d) for s, d in outs),
        in_specs=[pl.BlockSpec(memory_space=HBM if i in hbm else SMEM if i in smem else VMEM) for i in range(inputs)],
        out_specs=tuple(pl.BlockSpec(memory_space=HBM if i in hbm_out else VMEM) for i in range(len(outs))),
        scratch_shapes=scratch,
        name=name,
        compiler_params=pltpu.CompilerParams(vmem_limit_bytes=48 * 1024 * 1024),
    )
    return run


def rotated(x, axes, by):
    count = lax.axis_size(axes)
    return lax.ppermute(x, axes, [(i, (i + by) % count) for i in range(count)])


def body(raw, dead_mask, templates, assign, w_enc, b_enc, w_mid, b_mid, w_dec, b_dec, w_out, b_out):
    rows, length = raw.shape
    half = length // 2
    maps = w_enc.shape[0]
    chans = lax.axis_size("chan")
    blocks = lax.axis_size("tmpl")
    tmpl = templates.shape[0]
    small = [
        raw,
        dead_mask[None],
        w_enc.transpose(1, 2, 3, 0),
        w_mid.transpose(2, 3, 1, 0),
        w_dec.transpose(2, 3, 0, 1),
        b_enc[None],
        b_mid[None],
        b_dec[None],
        w_out[None],
    ]
    *loaded, first, second = call(
        load_kernel,
        [(x.shape, x.dtype) for x in small] + [((EDGE, length), BF)] * 2,
        [pltpu.SemaphoreType.DMA((len(small),))],
        hbm=range(len(small)),
        inputs=len(small),
        name="load",
    )(*small)
    r1 = lax.ppermute(first, "chan", [(i, i ^ 1) for i in range(chans) if i ^ 1 < chans])
    links = [(i, i + 1) for i in range(1, chans - 1, 2)]
    r2 = lax.ppermute(second, "chan", links + [(b, a) for a, b in links])

    dec_cols = (DEC_ROWS + 2) * 4 * maps + (DEC_ROWS // 2 + 2) * 6 * maps
    weights = call(
        prep_kernel,
        [
            ((ENC_ROWS * 4 * maps, 6 * (ENC_ROWS + EDGE)), BF),
            ((MID_ROWS * 2 * maps, (MID_ROWS + 2) * 3 * maps), BF),
            ((DEC_ROWS * 2 * maps, dec_cols), BF),
            ((2 * DEC_ROWS, DEC_ROWS * 2 * maps), BF),
            ((4 * maps, half), F32),
            ((2 * maps, half), F32),
            ((2 * maps, half), F32),
        ],
        [pltpu.VMEM((DEC_ROWS * 2 * maps, dec_cols), F32)],
        inputs=7,
        name="prep",
    )(*loaded[2:9])
    mid_groups = -(-(rows // 2 + 2) // MID_ROWS)
    (denoised,) = call(
        unet_kernel,
        [((rows, length), BF)],
        [
            pltpu.VMEM((6, rows + 2 * EDGE, half), F32),
            pltpu.VMEM(((rows + EDGE) * 4 * maps, half), BF),
            pltpu.VMEM(((mid_groups * MID_ROWS + 2) * 3 * maps, half), BF),
            pltpu.VMEM(((rows // 2 + 2) * 6 * maps, half), BF),
            pltpu.VMEM((rows, half), F32),
            pltpu.VMEM((rows, half), F32),
        ],
        smem=(11,),
        inputs=12,
        name="unet",
    )(*loaded[:2], r1, r2, *weights, b_out)

    forward = jnp.asarray(forward_table(length))
    inverse = jnp.asarray(inverse_table(length))
    gathered = [rotated(denoised, "tmpl", k) for k in range(1, blocks)]
    spectra = call(
        own_kernel,
        [((tmpl, rows, length), F32), ((tmpl, rows, length), F32), ((tmpl, rows, 128), F32), ((tmpl, 2 * length), F32)],
        [pltpu.SMEM((tmpl,), jnp.int32), pltpu.VMEM((rows, 2 * length), F32), pltpu.SemaphoreType.DMA],
        hbm=(3,),
        inputs=4,
        name="own",
    )(denoised, templates, forward, assign)
    width = length // chans
    pairs = tmpl * blocks
    copied, keep, send = call(
        functools.partial(corr_kernel, blocks - 1),
        [((rows, length), BF), ((chans, pairs, width), F32), ((chans, pairs, width), BF)],
        [
            pltpu.VMEM(((blocks - 1) * rows, 2 * length), F32),
            pltpu.VMEM((blocks, tmpl, 2 * length), F32),
            pltpu.VMEM((2, chans, pairs, width), F32),
            pltpu.SemaphoreType.DMA,
        ],
        hbm_out=(0,),
        inputs=blocks + 6,
        name="corr",
    )(denoised, *gathered, *spectra, forward, inverse)
    got = lax.ppermute(send, "chan", [(i, i ^ 1) for i in range(chans)])
    total, *parts = call(
        fold_kernel, [((pairs, width), F32)] + [((pairs, width), BF)] * (chans - 1), inputs=2, name="fold"
    )(keep, got)
    for k, part in enumerate(parts, 1):
        step = k // 2 * 4 + k % 2
        total = total + lax.ppermute(part, ("chan", "tm"), [(i, i ^ step) for i in range(2 * chans)]).astype(F32)
    return copied, total.reshape(tmpl, blocks, 1, width)


def solution(mesh):
    return jax.shard_map(
        body,
        mesh=mesh,
        in_specs=(
            P("chan", ("tmpl", "tm")),
            P("chan"),
            P("tmpl", "chan", None),
            P("tmpl"),
            P(),
            P(),
            P(),
            P(),
            P(),
            P(),
            P(),
            P(),
        ),
        out_specs=(P("chan", ("tmpl", "tm")), P("tmpl", None, "tm", "chan")),
        check_vma=False,
    )
```

```python
import functools
import math

import jax
import jax.numpy as jnp
import numpy as np
from jax import lax
from jax.experimental import pallas as pl
from jax.experimental.pallas import tpu as pltpu
from jax.sharding import PartitionSpec as P

BF = jnp.bfloat16
F32 = jnp.float32
EDGE = 8
ENC_ROWS = 8
MID_ROWS = 3
DEC_ROWS = 4
OUT_ROWS = 8
PAD = 16
OFF = -1e30


def frequency_order(patch_len):
    return np.concatenate([np.arange(0, patch_len, 2), np.arange(1, patch_len, 2)])


def forward_table(patch_len):
    s = np.arange(patch_len)[:, None]
    f = frequency_order(patch_len)[None, :]
    phase = ((s * f) % (2 * patch_len)).astype(np.float64) * (math.pi / patch_len)
    table = np.concatenate([np.cos(phase), np.sin(phase)], axis=1)
    table[:, patch_len] = 1.0 - 2.0 * (np.arange(patch_len) % 2)
    return table.astype(jnp.bfloat16)


def split_order(patch_len):
    return np.concatenate([np.arange(0, patch_len, 2), np.arange(1, patch_len, 2)])


def dot(a, b):
    return jnp.dot(a, b, preferred_element_type=F32)


def dot_nt(a, b):
    return lax.dot_general(a, b, (((1,), (1,)), ((), ())), preferred_element_type=F32)


def iota(shape, dim):
    return lax.broadcasted_iota(jnp.int32, shape, dim)


def column(row, count):
    m = row.shape[1]
    pick = iota((count, m), 0) % m == iota((count, m), 1)
    return jnp.sum(jnp.where(pick, row, 0.0), axis=1, keepdims=True)


def load_kernel(*refs):
    count = (len(refs) - 3) // 2
    sources = refs[:count]
    copies = refs[count : 2 * count]
    first_ref, second_ref, sems = refs[2 * count :]
    moves = [pltpu.make_async_copy(src, dst, sems.at[i]) for i, (src, dst) in enumerate(zip(sources, copies))]
    for move in moves:
        move.start()
    moves[0].wait()
    moves[1].wait()
    raw_ref, mask_ref = copies[:2]
    rows = raw_ref.shape[0]
    alive = column(mask_ref[...].astype(F32), rows)
    head = raw_ref[:EDGE].astype(F32) * alive[:EDGE]
    tail = raw_ref[rows - EDGE :].astype(F32) * alive[rows - EDGE :]
    odd = lax.axis_index("chan") % 2 == 1
    first_ref[...] = jnp.where(odd, head, tail).astype(BF)
    second_ref[...] = jnp.where(odd, tail, head).astype(BF)
    for move in moves[2:]:
        move.wait()


def thirds(x):
    high = x.astype(BF).astype(F32)
    middle = (x - high).astype(BF).astype(F32)
    return high, middle, x - high - middle


def prep_kernel(
    we_ref, wm_ref, wd_ref, be_ref, bm_ref, bd_ref, wo_ref, enc_ref, mid_ref, dec_ref, out_ref, bdec_ref, wide_ref
):
    maps = we_ref.shape[3]
    rows, cols = enc_ref.shape
    window = ENC_ROWS + EDGE
    spread = jnp.where(iota((rows, maps), 0) % maps == iota((rows, maps), 1), 1.0, 0.0).astype(BF)
    we = jnp.concatenate([we_ref[0, y].astype(F32) for y in range(3)], axis=0).astype(BF)
    taps = dot_nt(spread, we)
    row_id = iota((rows, cols), 0)
    col_id = iota((rows, cols), 1)
    q = row_id // maps % 4
    dy = col_id % window - row_id // (4 * maps) - (EDGE // 2 - 1)
    dx = col_id // window - q
    tap = jnp.where((dy >= 0) & (dy < 3) & (dx >= 0) & (dx < 3), dy * 3 + dx, -1)
    acc = jnp.zeros((rows, cols), F32)
    for t in range(9):
        acc = jnp.where(tap == t, taps[:, t : t + 1], acc)
    at = col_id - 6 * window
    for t, part in enumerate(thirds(column(be_ref[...], rows))):
        acc = jnp.where(at == t, part, acc)
    acc = jnp.where(((at == 3) & (q == 0)) | ((at == 4) & (q == 3)), OFF, acc)
    enc_ref[...] = acc.astype(BF)
    rows, cols = mid_ref.shape
    wide_ref[:rows, :cols] = jnp.zeros((rows, cols), F32)
    wm = wm_ref[...].astype(F32).reshape(9 * maps, 2 * maps).T
    for r in range(MID_ROWS):
        wide_ref[r * 2 * maps : (r + 1) * 2 * maps, r * 3 * maps : r * 3 * maps + 9 * maps] = wm
    acc = wide_ref[:rows, :cols]
    at = iota((rows, cols), 1) - (cols - PAD)
    for t, part in enumerate(thirds(column(bm_ref[...], rows))):
        acc = jnp.where(at == t, part, acc)
    mid_ref[...] = acc.astype(BF)
    wide_ref[...] = jnp.zeros(wide_ref.shape, F32)
    skip_cols = (DEC_ROWS + 2) * 4 * maps
    k = [[wd_ref[y, x].astype(F32) for x in range(3)] for y in range(3)]
    ws = [jnp.concatenate([k[y][x][:, 2 * maps :] for x in range(3)], axis=1) for y in range(3)]
    split = ((0,), (1, 2)), ((0, 1), (2,))
    wu = {}
    for r in range(2):
        for q in range(2):
            for a in range(2):
                wu[r, q, a] = jnp.concatenate(
                    [sum(k[y][x][:, : 2 * maps] for y in split[r][a] for x in split[q][b]) for b in range(2)], axis=1
                )
    for r in range(DEC_ROWS):
        for q in range(2):
            top = (r * 2 + q) * maps
            for y in range(3):
                left = ((r + y) * 4 + q) * maps
                wide_ref[top : top + maps, left : left + 3 * maps] = ws[y]
            for a in range(2):
                left = skip_cols + ((r + 1) // 2 + a) * 6 * maps + q * 2 * maps
                wide_ref[top : top + maps, left : left + 4 * maps] = wu[r % 2, q, a]
    dec_ref[...] = wide_ref[...].astype(BF)
    n = out_ref.shape[1]
    repeat = jnp.where(iota((maps, n), 1) % maps == iota((maps, n), 0), 1.0, 0.0).astype(BF)
    weights = dot(wo_ref[...], repeat)
    r_id = iota(out_ref.shape, 0)
    c_id = iota(out_ref.shape, 1)
    same = (c_id // (2 * maps) == r_id % OUT_ROWS) & (c_id // maps % 2 == r_id // OUT_ROWS)
    out_ref[...] = jnp.where(same, weights, 0.0).astype(BF)
    bdec_ref[...] = jnp.broadcast_to(column(bd_ref[...], 2 * maps), bdec_ref.shape)


def shifted(x, by):
    width = x.shape[1]
    lane = iota(x.shape, 1)
    edge = 0 if by < 0 else width - 1
    return jnp.where(lane == edge, 0.0, pltpu.roll(x, (-by) % width, 1))


def constants(half):
    row = iota((PAD, half), 0)
    lane = iota((PAD, half), 1)
    one = (row < 3) | ((row == 3) & (lane == 0)) | ((row == 4) & (lane == half - 1))
    return jnp.where(one, 1.0, 0.0).astype(BF)


def sixfold(even, uneven):
    return [shifted(even, -1), shifted(uneven, -1), even, uneven, shifted(even, 1), shifted(uneven, 1)]


def relu(y, keep=None):
    if keep is not None:
        y = y * keep
    return jnp.maximum(y.astype(BF), jnp.zeros((), BF))


def encode(weights, pieces, fixed, keeps, e4_ref, p3_ref):
    half = fixed.shape[1]
    window = jnp.concatenate([jnp.concatenate(pieces, axis=0).astype(BF), fixed], axis=0)
    y = dot(weights, window)
    span = y.shape[0] // ENC_ROWS
    maps = span // 4
    both = []
    for r in range(ENC_ROWS):
        piece = relu(y[r * span : (r + 1) * span], keeps[r])
        e4_ref[r * span : (r + 1) * span, :] = piece
        both.append(piece[maps : 3 * maps].astype(F32))
    for r in range(0, ENC_ROWS, 2):
        total = both[r] + both[r + 1]
        pooled = ((total[:maps] + total[maps:]) * 0.25).astype(BF).astype(F32)
        at = r // 2 * 3 * maps
        p3_ref[at : at + 3 * maps, :] = jnp.concatenate(
            [shifted(pooled, -1), pooled, shifted(pooled, 1)], axis=0
        ).astype(BF)


def inner_kernel(raw_ref, mask_ref, enc_ref, x_ref, perm_ref, e4_ref, p3_ref):
    rows, length = raw_ref.shape
    half = length // 2
    s = iota((length, half), 0)
    t = iota((length, half), 1)
    perm_ref[:, :half] = jnp.where(s == 2 * t, 1.0, 0.0).astype(BF)
    perm_ref[:, half:] = jnp.where(s == 2 * t + 1, 1.0, 0.0).astype(BF)
    alive = column(mask_ref[...].astype(F32), rows)
    x = dot((raw_ref[...].astype(F32) * alive).astype(BF), perm_ref[...])
    x_ref[...] = x
    six = sixfold(x[:, :half], x[:, half:])
    fixed = constants(half)
    span = enc_ref.shape[0] // ENC_ROWS
    pooled = span // 4 * 3 * ENC_ROWS // 2
    for g in range(rows // ENC_ROWS - 1):
        top = g * ENC_ROWS
        encode(
            enc_ref[...],
            [piece[top : top + ENC_ROWS + EDGE] for piece in six],
            fixed,
            [None] * ENC_ROWS,
            e4_ref.at[top * span : (top + ENC_ROWS) * span],
            p3_ref.at[g * pooled : (g + 1) * pooled],
        )


def rows_from(parts, low, high, span):
    found = []
    for first, stop, ref in parts:
        a, b = max(low, first), min(high, stop)
        if a < b:
            found.append(ref[(a - first) * span : (b - first) * span, :])
    return found


def unet_kernel(
    x_ref, mask_ref, perm_ref, r1_ref, r2_ref, e4_ref, p3_ref, enc_ref, mid_ref, dec_ref, wout_ref, bdec_ref, bout_ref,
    out_ref, e_top_ref, e_bottom_ref, p_top_ref, p_bottom_ref, m3_ref,
):
    rows, length = x_ref.shape
    half = length // 2
    span = enc_ref.shape[0] // ENC_ROWS
    maps = span // 4
    here = lax.axis_index("chan")
    last = lax.axis_size("chan") - 1
    odd = here % 2 == 1
    keep_top = jnp.where(here == 0, 0.0, 1.0)
    keep_bottom = jnp.where(here == last, 0.0, 1.0)
    alive = column(mask_ref[...].astype(F32), rows)
    r1 = r1_ref[...].astype(F32)
    r2 = r2_ref[...].astype(F32)
    edges = jnp.concatenate([jnp.where(odd, r1, r2), jnp.where(odd, r2, r1)], axis=0).astype(BF)
    edges = dot(edges, perm_ref[...])
    fixed = constants(half)
    margin = EDGE // 2
    for x, keeps, e_ref, p_ref in (
        (
            jnp.concatenate([edges[:EDGE], x_ref[:ENC_ROWS]], axis=0),
            [keep_top] * margin + [None] * (ENC_ROWS - margin),
            e_top_ref,
            p_top_ref,
        ),
        (
            jnp.concatenate([x_ref[rows - ENC_ROWS :], edges[EDGE:]], axis=0),
            [None] * (ENC_ROWS - margin) + [keep_bottom] * margin,
            e_bottom_ref,
            p_bottom_ref,
        ),
    ):
        encode(enc_ref[...], sixfold(x[:, :half], x[:, half:]), fixed, keeps, e_ref, p_ref)
    p_bottom_ref[ENC_ROWS // 2 * 3 * maps :, :] = jnp.zeros(
        (p_bottom_ref.shape[0] - ENC_ROWS // 2 * 3 * maps, half), BF
    )
    e4 = [(0, ENC_ROWS, e_top_ref), (ENC_ROWS, rows, e4_ref), (rows, rows + EDGE, e_bottom_ref)]
    few = ENC_ROWS // 2
    p3 = [(0, few, p_top_ref), (few, rows // 2, p3_ref), (rows // 2, rows // 2 + few + MID_ROWS, p_bottom_ref)]
    total = rows // 2 + 2
    span_m = 6 * maps
    for start in range(0, total, MID_ROWS):
        window = rows_from(p3, start, start + MID_ROWS + 2, 3 * maps)
        y = dot(mid_ref[...], jnp.concatenate(window + [fixed], axis=0))
        for r in range(min(MID_ROWS, total - start)):
            row = start + r
            keep = keep_top if row == 0 else keep_bottom if row == total - 1 else None
            piece = relu(y[r * 2 * maps : (r + 1) * 2 * maps], keep).astype(F32)
            m3_ref[row * span_m : (row + 1) * span_m, :] = jnp.concatenate(
                [shifted(piece, -1), piece, shifted(piece, 1)], axis=0
            ).astype(BF)
    m3 = [(0, total, m3_ref)]
    bias = jnp.concatenate([bdec_ref[...]] * DEC_ROWS, axis=0)
    for top in range(0, rows, OUT_ROWS):
        decoded = []
        for start in range(top, top + OUT_ROWS, DEC_ROWS):
            low = start + margin - 1
            window = rows_from(e4, low, low + DEC_ROWS + 2, span) + rows_from(
                m3, start // 2, start // 2 + DEC_ROWS // 2 + 2, span_m
            )
            decoded.append(relu(dot(dec_ref[...], jnp.concatenate(window, axis=0)) + bias))
        branch = dot(wout_ref[...], jnp.concatenate(decoded, axis=0))
        for q in range(2):
            own = x_ref[top : top + OUT_ROWS, q * half : (q + 1) * half]
            value = own + branch[q * OUT_ROWS : (q + 1) * OUT_ROWS] + bout_ref[0]
            out_ref[top : top + OUT_ROWS, q * half : (q + 1) * half] = (alive[top : top + OUT_ROWS] * value).astype(BF)


def products(spectra, ta_ref, tb_ref, tf_ref, put):
    tmpl, rows, length = ta_ref.shape
    count = len(spectra)
    for lane in range(0, length, 128):
        real = {}
        imag = {}
        for c in range(0, rows, 8):
            at = [ta_ref[r, c : c + 8, lane : lane + 128] for r in range(tmpl)]
            bt = [tb_ref[r, c : c + 8, lane : lane + 128] for r in range(tmpl)]
            af = at if lane else [tf_ref[r, c : c + 8, :] for r in range(tmpl)]
            for i in range(count):
                ax = spectra[i][c : c + 8, lane : lane + 128]
                bx = spectra[i][c : c + 8, length + lane : length + lane + 128]
                for r in range(tmpl):
                    re = ax * at[r] + bx * bt[r]
                    im = bx * af[r] - ax * bt[r]
                    real[r, i] = re if c == 0 else real[r, i] + re
                    imag[r, i] = im if c == 0 else imag[r, i] + im
        for r in range(tmpl):
            for i in range(count):
                put(r, i, lane, jnp.sum(real[r, i], axis=0, keepdims=True))
                put(r, i, length + lane, jnp.sum(imag[r, i], axis=0, keepdims=True))


def own_kernel(
    x_ref, t_ref, table_ref, split_ref, perm_ref, assign_ref,
    a_ref, b_ref, first_ref, p_ref, copy_ref, order_ref, s_ref, natural_ref, sems,
):
    fetch = pltpu.make_async_copy(assign_ref, order_ref, sems.at[0])
    fetch.start()
    natural_ref[...] = dot_nt(x_ref[...], perm_ref[...]).astype(BF)
    store = pltpu.make_async_copy(natural_ref, copy_ref, sems.at[1])
    store.start()
    tmpl, rows, length = t_ref.shape
    s_ref[...] = dot(x_ref[...], split_ref[...])
    fetch.wait()
    for r in range(tmpl):
        y = dot(t_ref[order_ref[r] % tmpl], table_ref[...])
        a = y[:, :length]
        b = y[:, length:]
        lane = iota((rows, 128), 1)
        a_ref[r] = a
        b_ref[r] = b
        b_ref[r, :, :128] = jnp.where(lane == 0, 0.0, b[:, :128])
        first_ref[r] = jnp.where(lane == 0, b[:, :128], a[:, :128])

    def put(r, i, lane, row):
        p_ref[r : r + 1, lane : lane + 128] = row

    products([s_ref], a_ref, b_ref, first_ref, put)
    store.wait()


def corr_kernel(others, *refs):
    x_refs = refs[:others]
    ta_ref, tb_ref, tf_ref, own_ref, table_ref, split_ref = refs[others : others + 6]
    keep_ref, send_ref, s_ref, p_ref, share_ref = refs[others + 6 :]
    count = others + 1
    tmpl, rows, length = ta_ref.shape
    here = lax.axis_index("tmpl")
    p_ref[here] = own_ref[...]
    if others:
        s_ref[...] = dot(jnp.concatenate([x_ref[...] for x_ref in x_refs], axis=0), split_ref[...])

    def put(r, i, lane, row):
        p_ref[(here + others - i) % count, r : r + 1, lane : lane + 128] = row

    products([s_ref.at[i * rows : (i + 1) * rows] for i in range(others)], ta_ref, tb_ref, tf_ref, put)
    p = jnp.concatenate([p_ref[i, r : r + 1, :] for r in range(tmpl) for i in range(count)], axis=0)
    lane = iota(p.shape, 1)
    p = jnp.where((lane == 0) | (lane == length), p * 0.5, p)
    high = p.astype(BF)
    low = (p - high.astype(F32)).astype(BF)
    pairs = tmpl * count
    both = jnp.concatenate([high, low], axis=0)
    half = length // 2

    def part(first):
        y = sum(dot_nt(both[:, at : at + half], table_ref[:, at : at + half]) for at in (first, length + first))
        return (y[:pairs] + y[pairs:]) * (1.0 / length)

    even = part(0)
    uneven = part(half)
    near = even + uneven
    far = even - uneven
    block = iota(far.shape, 0) % count
    later = jnp.where(block == count - 1, 0.0, pltpu.roll(far, pairs - 1, 0))
    parity = lax.axis_index("tm")
    far = jnp.where(parity == 1, far, later)
    width = share_ref.shape[3]
    chans = share_ref.shape[1]
    for c in range(chans):
        share_ref[0, c] = near[:, c * width : (c + 1) * width]
        share_ref[1, c] = far[:, c * width : (c + 1) * width]
    chan = lax.axis_index("chan")
    mine = chan // 2 * 2 + parity
    for k in range(chans):
        to = mine ^ k
        kind = (to + parity) % 2
        keep_ref[k] = share_ref[kind, to // 2 * 2 + chan % 2]
        send_ref[k] = share_ref[kind, to // 2 * 2 + 1 - chan % 2].astype(BF)


def fold_kernel(keep_ref, got_ref, own_ref, *outs):
    own_ref[...] = keep_ref[0] + got_ref[0].astype(F32)
    for k, out in enumerate(outs):
        out[...] = (keep_ref[k + 1] + got_ref[k + 1].astype(F32)).astype(BF)


VMEM = pltpu.MemorySpace.VMEM
HBM = pltpu.MemorySpace.HBM
SMEM = pltpu.MemorySpace.SMEM


def call(kernel, outs, scratch=(), hbm=(), smem=(), hbm_out=(), inputs=0, name=None):
    def run(*args):
        return inner(*[pltpu.with_memory_space_constraint(x, HBM) if i in hbm else x for i, x in enumerate(args)])

    inner = pl.pallas_call(
        kernel,
        out_shape=tuple(jax.ShapeDtypeStruct(s, d) for s, d in outs),
        in_specs=[pl.BlockSpec(memory_space=HBM if i in hbm else SMEM if i in smem else VMEM) for i in range(inputs)],
        out_specs=tuple(pl.BlockSpec(memory_space=HBM if i in hbm_out else VMEM) for i in range(len(outs))),
        scratch_shapes=scratch,
        name=name,
        compiler_params=pltpu.CompilerParams(vmem_limit_bytes=48 * 1024 * 1024),
    )
    return run


def rotated(x, axes, by):
    count = lax.axis_size(axes)
    return lax.ppermute(x, axes, [(i, (i + by) % count) for i in range(count)])


def body(raw, dead_mask, templates, assign, w_enc, b_enc, w_mid, b_mid, w_dec, b_dec, w_out, b_out):
    rows, length = raw.shape
    half = length // 2
    maps = w_enc.shape[0]
    chans = lax.axis_size("chan")
    blocks = lax.axis_size("tmpl")
    tmpl = templates.shape[0]
    small = [
        raw,
        dead_mask[None],
        w_enc.transpose(1, 2, 3, 0),
        w_mid.transpose(2, 3, 1, 0),
        w_dec.transpose(2, 3, 0, 1),
        b_enc[None],
        b_mid[None],
        b_dec[None],
        w_out[None],
    ]
    *loaded, first, second = call(
        load_kernel,
        [(x.shape, x.dtype) for x in small] + [((EDGE, length), BF)] * 2,
        [pltpu.SemaphoreType.DMA((len(small),))],
        hbm=range(len(small)),
        inputs=len(small),
        name="load",
    )(*small)
    r1 = lax.ppermute(first, "chan", [(i, i ^ 1) for i in range(chans) if i ^ 1 < chans])
    links = [(i, i + 1) for i in range(1, chans - 1, 2)]
    r2 = lax.ppermute(second, "chan", links + [(b, a) for a, b in links])

    dec_cols = (DEC_ROWS + 2) * 4 * maps + (DEC_ROWS // 2 + 2) * 6 * maps
    enc_w, mid_w, dec_w, out_w, dec_b = call(
        prep_kernel,
        [
            ((ENC_ROWS * 4 * maps, 6 * (ENC_ROWS + EDGE) + PAD), BF),
            ((MID_ROWS * 2 * maps, (MID_ROWS + 2) * 3 * maps + PAD), BF),
            ((DEC_ROWS * 2 * maps, dec_cols), BF),
            ((2 * OUT_ROWS, OUT_ROWS * 2 * maps), BF),
            ((2 * maps, half), F32),
        ],
        [pltpu.VMEM((DEC_ROWS * 2 * maps, dec_cols), F32)],
        inputs=7,
        name="prep",
    )(*loaded[2:9])
    x, perm, e4, p3 = call(
        inner_kernel,
        [
            ((rows, length), F32),
            ((length, length), BF),
            (((rows - ENC_ROWS) * 4 * maps, half), BF),
            (((rows - ENC_ROWS) // 2 * 3 * maps, half), BF),
        ],
        inputs=3,
        name="inner",
    )(*loaded[:2], enc_w)
    (denoised,) = call(
        unet_kernel,
        [((rows, length), BF)],
        [
            pltpu.VMEM((ENC_ROWS * 4 * maps, half), BF),
            pltpu.VMEM((ENC_ROWS * 4 * maps, half), BF),
            pltpu.VMEM((ENC_ROWS // 2 * 3 * maps, half), BF),
            pltpu.VMEM(((ENC_ROWS // 2 + MID_ROWS) * 3 * maps, half), BF),
            pltpu.VMEM(((rows // 2 + 2) * 6 * maps, half), BF),
        ],
        smem=(12,),
        inputs=13,
        name="unet",
    )(x, loaded[1], perm, r1, r2, e4, p3, enc_w, mid_w, dec_w, out_w, dec_b, b_out)

    forward = jnp.asarray(forward_table(length))
    split = jnp.asarray(forward_table(length)[split_order(length)])
    gathered = [rotated(denoised, "tmpl", k) for k in range(1, blocks)]
    *spectra, natural = call(
        own_kernel,
        [
            ((tmpl, rows, length), F32),
            ((tmpl, rows, length), F32),
            ((tmpl, rows, 128), F32),
            ((tmpl, 2 * length), F32),
            ((rows, length), BF),
        ],
        [
            pltpu.SMEM((tmpl,), jnp.int32),
            pltpu.VMEM((rows, 2 * length), F32),
            pltpu.VMEM((rows, length), BF),
            pltpu.SemaphoreType.DMA((2,)),
        ],
        hbm=(5,),
        hbm_out=(4,),
        inputs=6,
        name="own",
    )(denoised, templates, forward, split, perm, assign)
    width = length // chans
    pairs = tmpl * blocks
    keep, send = call(
        functools.partial(corr_kernel, blocks - 1),
        [((chans, pairs, width), F32), ((chans, pairs, width), BF)],
        [
            pltpu.VMEM(((blocks - 1) * rows, 2 * length), F32),
            pltpu.VMEM((blocks, tmpl, 2 * length), F32),
            pltpu.VMEM((2, chans, pairs, width), F32),
        ],
        inputs=blocks + 5,
        name="corr",
    )(*gathered, *spectra, forward, split)
    got = lax.ppermute(send, "chan", [(i, i ^ 1) for i in range(chans)])
    total, *parts = call(
        fold_kernel, [((pairs, width), F32)] + [((pairs, width), BF)] * (chans - 1), inputs=2, name="fold"
    )(keep, got)
    for k, part in enumerate(parts, 1):
        step = k // 2 * 4 + k % 2
        total = total + lax.ppermute(part, ("chan", "tm"), [(i, i ^ step) for i in range(2 * chans)]).astype(F32)
    return natural, total.reshape(tmpl, blocks, 1, width)


def solution(mesh):
    return jax.shard_map(
        body,
        mesh=mesh,
        in_specs=(
            P("chan", ("tmpl", "tm")),
            P("chan"),
            P("tmpl", "chan", None),
            P("tmpl"),
            P(),
            P(),
            P(),
            P(),
            P(),
            P(),
            P(),
            P(),
        ),
        out_specs=(P("chan", ("tmpl", "tm")), P("tmpl", None, "tm", "chan")),
        check_vma=False,
    )
```

```python
import functools
import math

import jax
import jax.numpy as jnp
import numpy as np
from jax import lax
from jax.experimental import pallas as pl
from jax.experimental.pallas import tpu as pltpu
from jax.sharding import PartitionSpec as P


BF = jnp.bfloat16
F32 = jnp.float32
EDGE = 8
ENC_ROWS = 8
MID_ROWS = 3
DEC_ROWS = 4
OUT_ROWS = 8
PAD = 16
OFF = -1e30


def frequency_order(patch_len):
    return np.concatenate([np.arange(0, patch_len, 2), np.arange(1, patch_len, 2)])


def forward_table(patch_len):
    s = np.arange(patch_len)[:, None]
    f = frequency_order(patch_len)[None, :]
    phase = ((s * f) % (2 * patch_len)).astype(np.float64) * (math.pi / patch_len)
    table = np.concatenate([np.cos(phase), np.sin(phase)], axis=1)
    table[:, patch_len] = 1.0 - 2.0 * (np.arange(patch_len) % 2)
    return table.astype(jnp.bfloat16)


def split_order(patch_len):
    return np.concatenate([np.arange(0, patch_len, 2), np.arange(1, patch_len, 2)])


def dot(a, b):
    return jnp.dot(a, b, preferred_element_type=F32)


def dot_nt(a, b):
    return lax.dot_general(a, b, (((1,), (1,)), ((), ())), preferred_element_type=F32)


def iota(shape, dim):
    return lax.broadcasted_iota(jnp.int32, shape, dim)


def column(row, count):
    m = row.shape[1]
    pick = iota((count, m), 0) % m == iota((count, m), 1)
    return jnp.sum(jnp.where(pick, row, 0.0), axis=1, keepdims=True)


def load_kernel(*refs):
    count = (len(refs) - 3) // 2
    sources = refs[:count]
    copies = refs[count : 2 * count]
    first_ref, second_ref, sems = refs[2 * count :]
    moves = [pltpu.make_async_copy(src, dst, sems.at[i]) for i, (src, dst) in enumerate(zip(sources, copies))]
    for move in moves:
        move.start()
    moves[0].wait()
    moves[1].wait()
    raw_ref, mask_ref = copies[:2]
    rows = raw_ref.shape[0]
    alive = column(mask_ref[...].astype(F32), rows)
    head = raw_ref[:EDGE].astype(F32) * alive[:EDGE]
    tail = raw_ref[rows - EDGE :].astype(F32) * alive[rows - EDGE :]
    odd = lax.axis_index("chan") % 2 == 1
    first_ref[...] = jnp.where(odd, head, tail).astype(BF)
    second_ref[...] = jnp.where(odd, tail, head).astype(BF)
    for move in moves[2:]:
        move.wait()


def thirds(x):
    high = x.astype(BF).astype(F32)
    middle = (x - high).astype(BF).astype(F32)
    return high, middle, x - high - middle


def prep_kernel(
    we_ref, wm_ref, wd_ref, be_ref, bm_ref, bd_ref, wo_ref, enc_ref, mid_ref, dec_ref, out_ref, bdec_ref, wide_ref
):
    maps = we_ref.shape[3]
    span = 4 * maps
    width = -(-enc_ref.shape[1] // 128) * 128
    window = ENC_ROWS + EDGE
    spread = jnp.where(iota((span, maps), 0) % maps == iota((span, maps), 1), 1.0, 0.0).astype(BF)
    we = jnp.concatenate([we_ref[0, y].astype(F32) for y in range(3)], axis=0).astype(BF)
    taps = dot_nt(spread, we)
    q = iota((span, width), 0) // maps
    col_id = iota((span, width), 1)
    dy = col_id % window - (EDGE // 2 - 1)
    dx = col_id // window - q
    tap = jnp.where((dy >= 0) & (dy < 3) & (dx >= 0) & (dx < 3), dy * 3 + dx, -1)
    band = jnp.zeros((span, width), F32)
    for t in range(9):
        band = jnp.where(tap == t, taps[:, t : t + 1], band)
    at = col_id - 6 * window
    fixed = jnp.zeros((span, width), F32)
    for t, part in enumerate(thirds(column(be_ref[...], span))):
        fixed = jnp.where(at == t, part, fixed)
    fixed = jnp.where(((at == 3) & (q == 0)) | ((at == 4) & (q == 3)), OFF, fixed)
    for r in range(ENC_ROWS):
        row = (pltpu.roll(band, r, 1) if r else band) + fixed
        enc_ref[r * span : (r + 1) * span, :] = row[:, : enc_ref.shape[1]].astype(BF)
    rows, cols = mid_ref.shape
    wide_ref[:rows, :cols] = jnp.zeros((rows, cols), F32)
    wm = wm_ref[...].astype(F32).reshape(9 * maps, 2 * maps).T
    for r in range(MID_ROWS):
        wide_ref[r * 2 * maps : (r + 1) * 2 * maps, r * 3 * maps : r * 3 * maps + 9 * maps] = wm
    acc = wide_ref[:rows, :cols]
    at = iota((rows, cols), 1) - (cols - PAD)
    for t, part in enumerate(thirds(column(bm_ref[...], rows))):
        acc = jnp.where(at == t, part, acc)
    mid_ref[...] = acc.astype(BF)
    wide_ref[...] = jnp.zeros(wide_ref.shape, F32)
    skip_cols = (DEC_ROWS + 2) * 4 * maps
    k = [[wd_ref[y, x].astype(F32) for x in range(3)] for y in range(3)]
    ws = [jnp.concatenate([k[y][x][:, 2 * maps :] for x in range(3)], axis=1) for y in range(3)]
    split = ((0,), (1, 2)), ((0, 1), (2,))
    wu = {}
    for r in range(2):
        for q in range(2):
            for a in range(2):
                wu[r, q, a] = jnp.concatenate(
                    [sum(k[y][x][:, : 2 * maps] for y in split[r][a] for x in split[q][b]) for b in range(2)], axis=1
                )
    for r in range(DEC_ROWS):
        for q in range(2):
            top = (r * 2 + q) * maps
            for y in range(3):
                left = ((r + y) * 4 + q) * maps
                wide_ref[top : top + maps, left : left + 3 * maps] = ws[y]
            for a in range(2):
                left = skip_cols + ((r + 1) // 2 + a) * 6 * maps + q * 2 * maps
                wide_ref[top : top + maps, left : left + 4 * maps] = wu[r % 2, q, a]
    dec_ref[...] = wide_ref[...].astype(BF)
    n = out_ref.shape[1]
    repeat = jnp.where(iota((maps, n), 1) % maps == iota((maps, n), 0), 1.0, 0.0).astype(BF)
    weights = dot(wo_ref[...], repeat)
    r_id = iota(out_ref.shape, 0)
    c_id = iota(out_ref.shape, 1)
    same = (c_id // (2 * maps) == r_id % OUT_ROWS) & (c_id // maps % 2 == r_id // OUT_ROWS)
    out_ref[...] = jnp.where(same, weights, 0.0).astype(BF)
    bdec_ref[...] = jnp.broadcast_to(column(bd_ref[...], 2 * maps), bdec_ref.shape)


def shifted(x, by):
    width = x.shape[1]
    lane = iota(x.shape, 1)
    edge = 0 if by < 0 else width - 1
    return jnp.where(lane == edge, 0.0, pltpu.roll(x, (-by) % width, 1))


def constants(half):
    row = iota((PAD, half), 0)
    lane = iota((PAD, half), 1)
    one = (row < 3) | ((row == 3) & (lane == 0)) | ((row == 4) & (lane == half - 1))
    return jnp.where(one, 1.0, 0.0).astype(BF)


def sixfold(even, uneven):
    return [shifted(even, -1), shifted(uneven, -1), even, uneven, shifted(even, 1), shifted(uneven, 1)]


def relu(y, keep=None):
    if keep is not None:
        y = y * keep
    return jnp.maximum(y.astype(BF), jnp.zeros((), BF))


def encode(weights, pieces, fixed, keeps, e4_ref, p3_ref):
    window = jnp.concatenate([jnp.concatenate(pieces, axis=0).astype(BF), fixed], axis=0)
    y = dot(weights, window)
    span = y.shape[0] // ENC_ROWS
    maps = span // 4
    both = []
    for r in range(ENC_ROWS):
        piece = relu(y[r * span : (r + 1) * span], keeps[r])
        e4_ref[r * span : (r + 1) * span, :] = piece
        both.append(piece[maps : 3 * maps].astype(F32))
    for r in range(0, ENC_ROWS, 2):
        total = both[r] + both[r + 1]
        pooled = ((total[:maps] + total[maps:]) * 0.25).astype(BF).astype(F32)
        at = r // 2 * 3 * maps
        p3_ref[at : at + 3 * maps, :] = jnp.concatenate(
            [shifted(pooled, -1), pooled, shifted(pooled, 1)], axis=0
        ).astype(BF)


def rows_from(parts, low, high, span):
    found = []
    for first, stop, ref in parts:
        a, b = max(low, first), min(high, stop)
        if a < b:
            found.append(ref[(a - first) * span : (b - first) * span, :])
    return found


def narrow(weights, parts, fixed, start, keeps, m3_ref, at):
    maps2 = weights.shape[0] // MID_ROWS
    window = rows_from(parts, start, start + MID_ROWS + 2, maps2 // 2 * 3)
    y = dot(weights, jnp.concatenate(window + [fixed], axis=0))
    for r, keep in enumerate(keeps):
        piece = relu(y[r * maps2 : (r + 1) * maps2], keep).astype(F32)
        m3_ref[(at + r) * 3 * maps2 : (at + r + 1) * 3 * maps2, :] = jnp.concatenate(
            [shifted(piece, -1), piece, shifted(piece, 1)], axis=0
        ).astype(BF)


def early_middle(rows):
    few = ENC_ROWS // 2
    first = -(-few // MID_ROWS)
    stop = (rows // 2 - MID_ROWS - 2) // MID_ROWS + 1
    return first, stop


def inner_kernel(raw_ref, mask_ref, enc_ref, mid_ref, x_ref, perm_ref, e4_ref, p3_ref, m3_ref):
    rows, length = raw_ref.shape
    half = length // 2
    s = iota((length, half), 0)
    t = iota((length, half), 1)
    perm_ref[:, :half] = jnp.where(s == 2 * t, 1.0, 0.0).astype(BF)
    perm_ref[:, half:] = jnp.where(s == 2 * t + 1, 1.0, 0.0).astype(BF)
    alive = column(mask_ref[...].astype(F32), rows)
    x = dot((raw_ref[...].astype(F32) * alive).astype(BF), perm_ref[...])
    x_ref[...] = x
    six = sixfold(x[:, :half], x[:, half:])
    fixed = constants(half)
    span = enc_ref.shape[0] // ENC_ROWS
    pooled = span // 4 * 3 * ENC_ROWS // 2
    for g in range(rows // ENC_ROWS - 1):
        top = g * ENC_ROWS
        encode(
            enc_ref[...],
            [piece[top : top + ENC_ROWS + EDGE] for piece in six],
            fixed,
            [None] * ENC_ROWS,
            e4_ref.at[top * span : (top + ENC_ROWS) * span],
            p3_ref.at[g * pooled : (g + 1) * pooled],
        )
    first, stop = early_middle(rows)
    parts = [(ENC_ROWS // 2, rows // 2, p3_ref)]
    for g in range(first, stop):
        narrow(mid_ref[...], parts, fixed, g * MID_ROWS, [None] * MID_ROWS, m3_ref, (g - first) * MID_ROWS)


def edge_kernel(
    x_ref, perm_ref, r1_ref, r2_ref, p3_ref, enc_ref, mid_ref,
    e_top_ref, e_bottom_ref, m_top_ref, m_bottom_ref, p_top_ref, p_bottom_ref,
):
    rows, length = x_ref.shape
    half = length // 2
    span = enc_ref.shape[0] // ENC_ROWS
    maps = span // 4
    here = lax.axis_index("chan")
    last = lax.axis_size("chan") - 1
    odd = here % 2 == 1
    keep_top = jnp.where(here == 0, 0.0, 1.0)
    keep_bottom = jnp.where(here == last, 0.0, 1.0)
    r1 = r1_ref[...].astype(F32)
    r2 = r2_ref[...].astype(F32)
    edges = jnp.concatenate([jnp.where(odd, r1, r2), jnp.where(odd, r2, r1)], axis=0).astype(BF)
    edges = dot(edges, perm_ref[...])
    fixed = constants(half)
    margin = EDGE // 2
    for x, keeps, e_ref, p_ref in (
        (
            jnp.concatenate([edges[:EDGE], x_ref[:ENC_ROWS]], axis=0),
            [keep_top] * margin + [None] * (ENC_ROWS - margin),
            e_top_ref,
            p_top_ref,
        ),
        (
            jnp.concatenate([x_ref[rows - ENC_ROWS :], edges[EDGE:]], axis=0),
            [None] * (ENC_ROWS - margin) + [keep_bottom] * margin,
            e_bottom_ref,
            p_bottom_ref,
        ),
    ):
        encode(enc_ref[...], sixfold(x[:, :half], x[:, half:]), fixed, keeps, e_ref, p_ref)
    p_bottom_ref[ENC_ROWS // 2 * 3 * maps :, :] = jnp.zeros(
        (p_bottom_ref.shape[0] - ENC_ROWS // 2 * 3 * maps, half), BF
    )
    few = ENC_ROWS // 2
    p3 = [(0, few, p_top_ref), (few, rows // 2, p3_ref), (rows // 2, rows // 2 + few + MID_ROWS, p_bottom_ref)]
    total = rows // 2 + 2
    first, stop = early_middle(rows)
    keeps = [keep_top] + [None] * (total - 2) + [keep_bottom]
    for g in range(-(-total // MID_ROWS)):
        start = g * MID_ROWS
        if g < first:
            narrow(mid_ref[...], p3, fixed, start, keeps[start : start + MID_ROWS], m_top_ref, start)
        elif g >= stop:
            narrow(
                mid_ref[...], p3, fixed, start, keeps[start : start + MID_ROWS], m_bottom_ref, start - stop * MID_ROWS
            )


def decode_kernel(
    x_ref, mask_ref, e_top_ref, e4_ref, e_bottom_ref, m_top_ref, m_ref, m_bottom_ref, dec_ref, wout_ref, bdec_ref, bout_ref,
    out_ref,
):
    rows, length = x_ref.shape
    half = length // 2
    span = bdec_ref.shape[0] * 2
    span_m = bdec_ref.shape[0] * 3
    total = rows // 2 + 2
    first, stop = early_middle(rows)
    e4 = [(0, ENC_ROWS, e_top_ref), (ENC_ROWS, rows, e4_ref), (rows, rows + EDGE, e_bottom_ref)]
    m3 = [
        (0, first * MID_ROWS, m_top_ref),
        (first * MID_ROWS, stop * MID_ROWS, m_ref),
        (stop * MID_ROWS, total, m_bottom_ref),
    ]
    alive = column(mask_ref[...].astype(F32), rows)
    bias = jnp.concatenate([bdec_ref[...]] * DEC_ROWS, axis=0)
    depth = half
    steps = dec_ref.shape[1] // depth
    units = OUT_ROWS // DEC_ROWS
    tiles = DEC_ROWS * bdec_ref.shape[0] * units // depth

    def finish(*accs):
        sums = [accs[:units], accs[units : 2 * units]]
        outs = accs[2 * units :]
        turn = [0] * units
        waiting = None

        def push(tile, unit):
            slot = turn[unit] % 2
            turn[unit] += 1
            pltpu.matmul_push_rhs(tile, slot, unit)
            return slot

        def project(item):
            top, decoded = item
            unit = top // OUT_ROWS % units
            for k in range(tiles):
                slot = push(decoded[k * depth : (k + 1) * depth], unit)
                pltpu.matmul_acc_lhs(outs[unit], wout_ref[:, k * depth : (k + 1) * depth], load_staged_rhs=slot)
            branch = pltpu.matmul_pop(outs[unit])
            for q in range(2):
                own = x_ref[top : top + OUT_ROWS, q * half : (q + 1) * half]
                value = own + branch[q * OUT_ROWS : (q + 1) * OUT_ROWS] + bout_ref[0]
                out_ref[top : top + OUT_ROWS, q * half : (q + 1) * half] = (
                    alive[top : top + OUT_ROWS] * value
                ).astype(BF)

        for top in range(0, rows, OUT_ROWS):
            windows = []
            for start in range(top, top + OUT_ROWS, DEC_ROWS):
                low = start + EDGE // 2 - 1
                windows.append(
                    jnp.concatenate(
                        rows_from(e4, low, low + DEC_ROWS + 2, span)
                        + rows_from(m3, start // 2, start // 2 + DEC_ROWS // 2 + 2, span_m),
                        axis=0,
                    )
                )
            now = sums[top // OUT_ROWS % 2]
            for k in range(steps):
                slots = [push(w[k * depth : (k + 1) * depth], unit) for unit, w in enumerate(windows)]
                for acc, slot in zip(now, slots):
                    pltpu.matmul_acc_lhs(acc, dec_ref[:, k * depth : (k + 1) * depth], load_staged_rhs=slot)
            if waiting:
                project(waiting)
            waiting = top, jnp.concatenate([relu(pltpu.matmul_pop(acc) + bias) for acc in now], axis=0)
        project(waiting)

    pl.run_scoped(
        finish,
        *(pltpu.ACC(unit)((dec_ref.shape[0], half), F32) for _ in range(2) for unit in range(units)),
        *(pltpu.ACC(unit)((wout_ref.shape[0], half), F32) for unit in range(units)),
    )


def products(spectra, ta_ref, tb_ref, tf_ref, put):
    tmpl, rows, length = ta_ref.shape
    count = len(spectra)
    for lane in range(0, length, 128):
        real = {}
        imag = {}
        for c in range(0, rows, 8):
            at = [ta_ref[r, c : c + 8, lane : lane + 128] for r in range(tmpl)]
            bt = [tb_ref[r, c : c + 8, lane : lane + 128] for r in range(tmpl)]
            af = at if lane else [tf_ref[r, c : c + 8, :] for r in range(tmpl)]
            for i in range(count):
                ax = spectra[i][c : c + 8, lane : lane + 128]
                bx = spectra[i][c : c + 8, length + lane : length + lane + 128]
                for r in range(tmpl):
                    re = ax * at[r] + bx * bt[r]
                    im = bx * af[r] - ax * bt[r]
                    real[r, i] = re if c == 0 else real[r, i] + re
                    imag[r, i] = im if c == 0 else imag[r, i] + im
        for r in range(tmpl):
            for i in range(count):
                put(r, i, lane, jnp.sum(real[r, i], axis=0, keepdims=True))
                put(r, i, length + lane, jnp.sum(imag[r, i], axis=0, keepdims=True))


def own_kernel(
    x_ref, t_ref, table_ref, split_ref, perm_ref, assign_ref,
    a_ref, b_ref, first_ref, p_ref, copy_ref, order_ref, s_ref, natural_ref, sems,
):
    fetch = pltpu.make_async_copy(assign_ref, order_ref, sems.at[0])
    fetch.start()
    natural_ref[...] = dot_nt(x_ref[...], perm_ref[...]).astype(BF)
    store = pltpu.make_async_copy(natural_ref, copy_ref, sems.at[1])
    store.start()
    tmpl, rows, length = t_ref.shape
    s_ref[...] = dot(x_ref[...], split_ref[...])
    fetch.wait()
    for r in range(tmpl):
        y = dot(t_ref[order_ref[r] % tmpl], table_ref[...])
        a = y[:, :length]
        b = y[:, length:]
        lane = iota((rows, 128), 1)
        a_ref[r] = a
        b_ref[r] = b
        b_ref[r, :, :128] = jnp.where(lane == 0, 0.0, b[:, :128])
        first_ref[r] = jnp.where(lane == 0, b[:, :128], a[:, :128])

    def put(r, i, lane, row):
        p_ref[r : r + 1, lane : lane + 128] = row

    products([s_ref], a_ref, b_ref, first_ref, put)
    store.wait()


def other_kernel(x_ref, ta_ref, tb_ref, tf_ref, split_ref, p_ref, s_ref):
    s_ref[...] = dot(x_ref[...], split_ref[...])

    def put(r, i, lane, row):
        p_ref[r : r + 1, lane : lane + 128] = row

    products([s_ref], ta_ref, tb_ref, tf_ref, put)


def corr_kernel(count, *refs):
    part_refs = refs[: count - 1]
    x_ref, ta_ref, tb_ref, tf_ref, table_ref, split_ref = refs[count - 1 : count + 5]
    keep_ref, send_ref, s_ref, p_ref, share_ref = refs[count + 5 :]
    tmpl, _, length = ta_ref.shape
    here = lax.axis_index("tmpl")
    for i, part_ref in enumerate(part_refs):
        p_ref[(here - i) % count] = part_ref[...]
    s_ref[...] = dot(x_ref[...], split_ref[...])

    def put(r, i, lane, row):
        p_ref[(here + 1) % count, r : r + 1, lane : lane + 128] = row

    products([s_ref], ta_ref, tb_ref, tf_ref, put)
    p = jnp.concatenate([p_ref[i, r : r + 1, :] for r in range(tmpl) for i in range(count)], axis=0)
    lane = iota(p.shape, 1)
    p = jnp.where((lane == 0) | (lane == length), p * 0.5, p)
    high = p.astype(BF)
    low = (p - high.astype(F32)).astype(BF)
    pairs = tmpl * count
    both = jnp.concatenate([high, low], axis=0)
    half = length // 2

    def part(first):
        y = sum(dot_nt(both[:, at : at + half], table_ref[:, at : at + half]) for at in (first, length + first))
        return (y[:pairs] + y[pairs:]) * (1.0 / length)

    even = part(0)
    uneven = part(half)
    near = even + uneven
    far = even - uneven
    block = iota(far.shape, 0) % count
    later = jnp.where(block == count - 1, 0.0, pltpu.roll(far, pairs - 1, 0))
    parity = lax.axis_index("tm")
    far = jnp.where(parity == 1, far, later)
    width = share_ref.shape[3]
    chans = share_ref.shape[1]
    for c in range(chans):
        share_ref[0, c] = near[:, c * width : (c + 1) * width]
        share_ref[1, c] = far[:, c * width : (c + 1) * width]
    chan = lax.axis_index("chan")
    mine = chan // 2 * 2 + parity
    for k in range(chans):
        to = mine ^ k
        kind = (to + parity) % 2
        keep_ref[k] = share_ref[kind, to // 2 * 2 + chan % 2]
        send_ref[k] = share_ref[kind, to // 2 * 2 + 1 - chan % 2].astype(BF)


def fold_kernel(keep_ref, got_ref, own_ref, *outs):
    own_ref[...] = keep_ref[0] + got_ref[0].astype(F32)
    for k, out in enumerate(outs):
        out[...] = (keep_ref[k + 1] + got_ref[k + 1].astype(F32)).astype(BF)


VMEM = pltpu.MemorySpace.VMEM
HBM = pltpu.MemorySpace.HBM
SMEM = pltpu.MemorySpace.SMEM


def call(kernel, outs, scratch=(), hbm=(), smem=(), hbm_out=(), inputs=0):
    def run(*args):
        return inner(*[pltpu.with_memory_space_constraint(x, HBM) if i in hbm else x for i, x in enumerate(args)])

    inner = pl.pallas_call(
        kernel,
        out_shape=tuple(jax.ShapeDtypeStruct(s, d) for s, d in outs),
        in_specs=[pl.BlockSpec(memory_space=HBM if i in hbm else SMEM if i in smem else VMEM) for i in range(inputs)],
        out_specs=tuple(pl.BlockSpec(memory_space=HBM if i in hbm_out else VMEM) for i in range(len(outs))),
        scratch_shapes=scratch,
        compiler_params=pltpu.CompilerParams(vmem_limit_bytes=48 * 1024 * 1024),
    )
    return run


def rotated(x, axes, by):
    count = lax.axis_size(axes)
    return lax.ppermute(x, axes, [(i, (i + by) % count) for i in range(count)])


def body(raw, dead_mask, templates, assign, w_enc, b_enc, w_mid, b_mid, w_dec, b_dec, w_out, b_out):
    rows, length = raw.shape
    half = length // 2
    maps = w_enc.shape[0]
    chans = lax.axis_size("chan")
    blocks = lax.axis_size("tmpl")
    tmpl = templates.shape[0]
    small = [
        raw,
        dead_mask[None],
        w_enc.transpose(1, 2, 3, 0),
        w_mid.transpose(2, 3, 1, 0),
        w_dec.transpose(2, 3, 0, 1),
        b_enc[None],
        b_mid[None],
        b_dec[None],
        w_out[None],
    ]
    *loaded, send1, send2 = call(
        load_kernel,
        [(x.shape, x.dtype) for x in small] + [((EDGE, length), BF)] * 2,
        [pltpu.SemaphoreType.DMA((len(small),))],
        hbm=range(len(small)),
        inputs=len(small),
    )(*small)
    r1 = lax.ppermute(send1, "chan", [(i, i ^ 1) for i in range(chans) if i ^ 1 < chans])
    links = [(i, i + 1) for i in range(1, chans - 1, 2)]
    r2 = lax.ppermute(send2, "chan", links + [(b, a) for a, b in links])

    dec_cols = (DEC_ROWS + 2) * 4 * maps + (DEC_ROWS // 2 + 2) * 6 * maps
    enc_w, mid_w, dec_w, out_w, dec_b = call(
        prep_kernel,
        [
            ((ENC_ROWS * 4 * maps, 6 * (ENC_ROWS + EDGE) + PAD), BF),
            ((MID_ROWS * 2 * maps, (MID_ROWS + 2) * 3 * maps + PAD), BF),
            ((DEC_ROWS * 2 * maps, dec_cols), BF),
            ((2 * OUT_ROWS, OUT_ROWS * 2 * maps), BF),
            ((2 * maps, half), F32),
        ],
        [pltpu.VMEM((DEC_ROWS * 2 * maps, dec_cols), F32)],
        inputs=7,
    )(*loaded[2:9])
    first, stop = early_middle(rows)
    x, perm, e4, p3, m3 = call(
        inner_kernel,
        [
            ((rows, length), F32),
            ((length, length), BF),
            (((rows - ENC_ROWS) * 4 * maps, half), BF),
            (((rows - ENC_ROWS) // 2 * 3 * maps, half), BF),
            (((stop - first) * MID_ROWS * 6 * maps, half), BF),
        ],
        inputs=4,
    )(*loaded[:2], enc_w, mid_w)
    e_top, e_bottom, m_top, m_bottom = call(
        edge_kernel,
        [
            ((ENC_ROWS * 4 * maps, half), BF),
            ((ENC_ROWS * 4 * maps, half), BF),
            ((first * MID_ROWS * 6 * maps, half), BF),
            (((rows // 2 + 2 - stop * MID_ROWS) * 6 * maps, half), BF),
        ],
        [
            pltpu.VMEM((ENC_ROWS // 2 * 3 * maps, half), BF),
            pltpu.VMEM(((ENC_ROWS // 2 + MID_ROWS) * 3 * maps, half), BF),
        ],
        inputs=7,
    )(x, perm, r1, r2, p3, enc_w, mid_w)
    (denoised,) = call(
        decode_kernel, [((rows, length), BF)], smem=(11,), inputs=12
    )(x, loaded[1], e_top, e4, e_bottom, m_top, m3, m_bottom, dec_w, out_w, dec_b, b_out)

    forward = jnp.asarray(forward_table(length))
    split = jnp.asarray(forward_table(length)[split_order(length)])
    gathered = []
    for k in range(1, blocks):
        gathered.append(rotated(denoised, "tmpl", k))
    *spectra, natural = call(
        own_kernel,
        [
            ((tmpl, rows, length), F32),
            ((tmpl, rows, length), F32),
            ((tmpl, rows, 128), F32),
            ((tmpl, 2 * length), F32),
            ((rows, length), BF),
        ],
        [
            pltpu.SMEM((tmpl,), jnp.int32),
            pltpu.VMEM((rows, 2 * length), F32),
            pltpu.VMEM((rows, length), BF),
            pltpu.SemaphoreType.DMA((2,)),
        ],
        hbm=(5,),
        hbm_out=(4,),
        inputs=6,
    )(denoised, templates, forward, split, perm, assign)
    width = length // chans
    pairs = tmpl * blocks
    sums = [spectra.pop()]
    for x in gathered[:-1]:
        (more,) = call(
            other_kernel, [((tmpl, 2 * length), F32)], [pltpu.VMEM((rows, 2 * length), F32)], inputs=5
        )(x, *spectra, split)
        sums.append(more)
    keep, send = call(
        functools.partial(corr_kernel, blocks),
        [((chans, pairs, width), F32), ((chans, pairs, width), BF)],
        [
            pltpu.VMEM((rows, 2 * length), F32),
            pltpu.VMEM((blocks, tmpl, 2 * length), F32),
            pltpu.VMEM((2, chans, pairs, width), F32),
        ],
        inputs=blocks + 5,
    )(*sums, gathered[-1], *spectra, forward, split)
    got = lax.ppermute(send, "chan", [(i, i ^ 1) for i in range(chans)])
    total, *parts = call(
        fold_kernel, [((pairs, width), F32)] + [((pairs, width), BF)] * (chans - 1), inputs=2
    )(keep, got)
    for k, part in enumerate(parts, 1):
        step = k // 2 * 4 + k % 2
        got = lax.ppermute(part, ("chan", "tm"), [(i, i ^ step) for i in range(2 * chans)])
        total = total + got.astype(F32)
    return natural, total.reshape(tmpl, blocks, 1, width)


def solution(mesh):
    return jax.shard_map(
        body,
        mesh=mesh,
        in_specs=(
            P("chan", ("tmpl", "tm")),
            P("chan"),
            P("tmpl", "chan", None),
            P("tmpl"),
            P(),
            P(),
            P(),
            P(),
            P(),
            P(),
            P(),
            P(),
        ),
        out_specs=(P("chan", ("tmpl", "tm")), P("tmpl", None, "tm", "chan")),
        check_vma=False,
    )
```

```python
import functools
import math

import jax
import jax.numpy as jnp
import numpy as np
from jax import lax
from jax.experimental import pallas as pl
from jax.experimental.pallas import tpu as pltpu
from jax.sharding import PartitionSpec as P


BF = jnp.bfloat16
F32 = jnp.float32
EDGE = 8
ENC_ROWS = 8
MID_ROWS = 3
DEC_ROWS = 4
OUT_ROWS = 8
PAD = 16


def frequency_order(patch_len):
    return np.concatenate([np.arange(0, patch_len, 2), np.arange(1, patch_len, 2)])


def forward_table(patch_len):
    s = np.arange(patch_len)[:, None]
    f = frequency_order(patch_len)[None, :]
    phase = ((s * f) % (2 * patch_len)).astype(np.float64) * (math.pi / patch_len)
    table = np.concatenate([np.cos(phase), np.sin(phase)], axis=1)
    table[:, patch_len] = 1.0 - 2.0 * (np.arange(patch_len) % 2)
    return table.astype(jnp.bfloat16)


def split_order(patch_len):
    return np.concatenate([np.arange(0, patch_len, 2), np.arange(1, patch_len, 2)])


def dot(a, b):
    return jnp.dot(a, b, preferred_element_type=F32)


def dot_nt(a, b):
    return lax.dot_general(a, b, (((1,), (1,)), ((), ())), preferred_element_type=F32)


def iota(shape, dim):
    return lax.broadcasted_iota(jnp.int32, shape, dim)


def column(row, count):
    m = row.shape[1]
    pick = iota((count, m), 0) % m == iota((count, m), 1)
    return jnp.sum(jnp.where(pick, row, 0.0), axis=1, keepdims=True)


def load_kernel(*refs):
    count = (len(refs) - 4) // 2
    sources = refs[:count]
    copies = refs[count : 2 * count]
    first_ref, second_ref, perm_ref, sems = refs[2 * count :]
    moves = [pltpu.make_async_copy(src, dst, sems.at[i]) for i, (src, dst) in enumerate(zip(sources, copies))]
    for move in moves:
        move.start()
    length = perm_ref.shape[0]
    half = length // 2
    s = iota((length, half), 0)
    t = iota((length, half), 1)
    perm_ref[:, :half] = jnp.where(s == 2 * t, 1.0, 0.0).astype(BF)
    perm_ref[:, half:] = jnp.where(s == 2 * t + 1, 1.0, 0.0).astype(BF)
    moves[0].wait()
    moves[1].wait()
    raw_ref, mask_ref = copies[:2]
    rows = raw_ref.shape[0]
    alive = column(mask_ref[...].astype(F32), rows)
    head = raw_ref[:EDGE].astype(F32) * alive[:EDGE]
    tail = raw_ref[rows - EDGE :].astype(F32) * alive[rows - EDGE :]
    odd = lax.axis_index("chan") % 2 == 1
    first_ref[...] = jnp.where(odd, head, tail).astype(BF)
    second_ref[...] = jnp.where(odd, tail, head).astype(BF)
    for move in moves[2:]:
        move.wait()


def thirds(x):
    high = x.astype(BF).astype(F32)
    middle = (x - high).astype(BF).astype(F32)
    return high, middle, x - high - middle


def prep_kernel(
    we_ref, wm_ref, wd_ref, be_ref, bm_ref, bd_ref, wo_ref, enc_ref, mid_ref, dec_ref, out_ref, bdec_ref, wide_ref
):
    maps = we_ref.shape[3]
    span = 2 * maps
    width = -(-enc_ref.shape[1] // 128) * 128
    window = ENC_ROWS + EDGE
    spread = jnp.where(iota((span, maps), 0) % maps == iota((span, maps), 1), 1.0, 0.0).astype(BF)
    we = jnp.concatenate([we_ref[0, y].astype(F32) for y in range(3)], axis=0).astype(BF)
    taps = dot_nt(spread, we)
    q = iota((span, width), 0) // maps
    col_id = iota((span, width), 1)
    dy = col_id % window - (EDGE // 2 - 1)
    dx = col_id // window - q
    tap = jnp.where((dy >= 0) & (dy < 3) & (dx >= 0) & (dx < 3), dy * 3 + dx, -1)
    band = jnp.zeros((span, width), F32)
    for t in range(9):
        band = jnp.where(tap == t, taps[:, t : t + 1], band)
    at = col_id - 4 * window
    fixed = jnp.zeros((span, width), F32)
    for t, part in enumerate(thirds(column(be_ref[...], span))):
        fixed = jnp.where(at == t, part, fixed)
    for r in range(ENC_ROWS):
        row = (pltpu.roll(band, r, 1) if r else band) + fixed
        enc_ref[r * span : (r + 1) * span, :] = row[:, : enc_ref.shape[1]].astype(BF)
    rows, cols = mid_ref.shape
    wide_ref[:rows, :cols] = jnp.zeros((rows, cols), F32)
    wm = wm_ref[...].astype(F32).reshape(9 * maps, 2 * maps).T
    for r in range(MID_ROWS):
        wide_ref[r * 2 * maps : (r + 1) * 2 * maps, r * 3 * maps : r * 3 * maps + 9 * maps] = wm
    acc = wide_ref[:rows, :cols]
    at = iota((rows, cols), 1) - (cols - PAD)
    for t, part in enumerate(thirds(column(bm_ref[...], rows))):
        acc = jnp.where(at == t, part, acc)
    mid_ref[...] = acc.astype(BF)
    wide_ref[...] = jnp.zeros(wide_ref.shape, F32)
    skip_cols = (DEC_ROWS + 2) * 4 * maps
    k = [[wd_ref[y, x].astype(F32) for x in range(3)] for y in range(3)]
    ws = [jnp.concatenate([k[y][x][:, 2 * maps :] for x in range(3)], axis=1) for y in range(3)]
    split = ((0,), (1, 2)), ((0, 1), (2,))
    wu = {}
    for r in range(2):
        for q in range(2):
            for a in range(2):
                wu[r, q, a] = jnp.concatenate(
                    [sum(k[y][x][:, : 2 * maps] for y in split[r][a] for x in split[q][b]) for b in range(2)], axis=1
                )
    for r in range(DEC_ROWS):
        for q in range(2):
            top = (r * 2 + q) * maps
            for y in range(3):
                left = ((r + y) * 4 + q) * maps
                wide_ref[top : top + maps, left : left + 3 * maps] = ws[y]
            for a in range(2):
                left = skip_cols + ((r + 1) // 2 + a) * 6 * maps + q * 2 * maps
                wide_ref[top : top + maps, left : left + 4 * maps] = wu[r % 2, q, a]
    dec_ref[...] = wide_ref[...].astype(BF)
    n = out_ref.shape[1]
    repeat = jnp.where(iota((maps, n), 1) % maps == iota((maps, n), 0), 1.0, 0.0).astype(BF)
    weights = dot(wo_ref[...], repeat)
    r_id = iota(out_ref.shape, 0)
    c_id = iota(out_ref.shape, 1)
    same = (c_id // (2 * maps) == r_id % OUT_ROWS) & (c_id // maps % 2 == r_id // OUT_ROWS)
    out_ref[...] = jnp.where(same, weights, 0.0).astype(BF)
    bdec_ref[...] = jnp.broadcast_to(column(bd_ref[...], 2 * maps), bdec_ref.shape)


def shifted(x, by):
    width = x.shape[1]
    moved = pltpu.roll(x, (-by) % width, 1)
    cut = width // 2
    parts = [moved[:, :cut], moved[:, cut:]]
    at = 0 if by < 0 else 1
    edge = iota(parts[at].shape, 1) == (0 if by < 0 else width - cut - 1)
    parts[at] = jnp.where(edge, jnp.zeros((), x.dtype), parts[at])
    return jnp.concatenate(parts, axis=1)


def constants(half):
    return jnp.where(iota((PAD, half), 0) < 3, 1.0, 0.0).astype(BF)


def fourfold(even, uneven):
    return [shifted(uneven, -1), even, uneven, shifted(even, 1)]


def relu(y, keep=None):
    if keep is not None:
        y = y * keep
    return jnp.maximum(y.astype(BF), jnp.zeros((), BF))


def encode(weights, pieces, fixed, keeps, e4_ref, p3_ref):
    window = jnp.concatenate([jnp.concatenate(pieces, axis=0).astype(BF), fixed], axis=0)
    y = dot(weights, window)
    span = y.shape[0] // ENC_ROWS
    maps = span // 2
    both = []
    for r in range(ENC_ROWS):
        piece = relu(y[r * span : (r + 1) * span], keeps[r])
        e4_ref[r * 2 * span : (r + 1) * 2 * span, :] = jnp.concatenate(fourfold(piece[:maps], piece[maps:]), axis=0)
        both.append(piece.astype(F32))
    for r in range(0, ENC_ROWS, 2):
        total = both[r] + both[r + 1]
        pooled = ((total[:maps] + total[maps:]) * 0.25).astype(BF)
        at = r // 2 * 3 * maps
        p3_ref[at : at + 3 * maps, :] = jnp.concatenate(
            [shifted(pooled, -1), pooled, shifted(pooled, 1)], axis=0
        )


def rows_from(parts, low, high, span):
    found = []
    for first, stop, ref in parts:
        a, b = max(low, first), min(high, stop)
        if a < b:
            found.append(ref[(a - first) * span : (b - first) * span, :])
    return found


def narrow(weights, parts, fixed, start, keeps, m3_ref, at):
    maps2 = weights.shape[0] // MID_ROWS
    window = rows_from(parts, start, start + MID_ROWS + 2, maps2 // 2 * 3)
    y = dot(weights, jnp.concatenate(window + [fixed], axis=0))
    for r, keep in enumerate(keeps):
        piece = relu(y[r * maps2 : (r + 1) * maps2], keep)
        m3_ref[(at + r) * 3 * maps2 : (at + r + 1) * 3 * maps2, :] = jnp.concatenate(
            [shifted(piece, -1), piece, shifted(piece, 1)], axis=0
        )


def early_middle(rows):
    few = ENC_ROWS // 2
    first = -(-few // MID_ROWS)
    stop = (rows // 2 - MID_ROWS - 2) // MID_ROWS + 1
    return first, stop


def inner_kernel(raw_ref, mask_ref, perm_ref, enc_ref, mid_ref, x_ref, e4_ref, p3_ref, m3_ref):
    rows, length = raw_ref.shape
    half = length // 2
    alive = column(mask_ref[...].astype(F32), rows)
    x = dot((raw_ref[...].astype(F32) * alive).astype(BF), perm_ref[...])
    x_ref[...] = x
    four = fourfold(x[:, :half], x[:, half:])
    fixed = constants(half)
    maps = enc_ref.shape[0] // ENC_ROWS // 2
    span = 4 * maps
    pooled = 3 * maps * ENC_ROWS // 2
    for g in range(rows // ENC_ROWS - 1):
        top = g * ENC_ROWS
        encode(
            enc_ref[...],
            [piece[top : top + ENC_ROWS + EDGE] for piece in four],
            fixed,
            [None] * ENC_ROWS,
            e4_ref.at[top * span : (top + ENC_ROWS) * span],
            p3_ref.at[g * pooled : (g + 1) * pooled],
        )
    first, stop = early_middle(rows)
    parts = [(ENC_ROWS // 2, rows // 2, p3_ref)]
    for g in range(first, stop):
        narrow(mid_ref[...], parts, fixed, g * MID_ROWS, [None] * MID_ROWS, m3_ref, (g - first) * MID_ROWS)


def edge_kernel(
    x_ref, perm_ref, r1_ref, r2_ref, p3_ref, enc_ref, mid_ref,
    e_top_ref, e_bottom_ref, m_top_ref, m_bottom_ref, p_top_ref, p_bottom_ref,
):
    rows, length = x_ref.shape
    half = length // 2
    maps = enc_ref.shape[0] // ENC_ROWS // 2
    here = lax.axis_index("chan")
    last = lax.axis_size("chan") - 1
    odd = here % 2 == 1
    keep_top = jnp.where(here == 0, 0.0, 1.0)
    keep_bottom = jnp.where(here == last, 0.0, 1.0)
    r1 = r1_ref[...].astype(F32)
    r2 = r2_ref[...].astype(F32)
    edges = jnp.concatenate([jnp.where(odd, r1, r2), jnp.where(odd, r2, r1)], axis=0).astype(BF)
    edges = dot(edges, perm_ref[...])
    fixed = constants(half)
    margin = EDGE // 2
    for x, keeps, e_ref, p_ref in (
        (
            jnp.concatenate([edges[:EDGE], x_ref[:ENC_ROWS]], axis=0),
            [keep_top] * margin + [None] * (ENC_ROWS - margin),
            e_top_ref,
            p_top_ref,
        ),
        (
            jnp.concatenate([x_ref[rows - ENC_ROWS :], edges[EDGE:]], axis=0),
            [None] * (ENC_ROWS - margin) + [keep_bottom] * margin,
            e_bottom_ref,
            p_bottom_ref,
        ),
    ):
        encode(enc_ref[...], fourfold(x[:, :half], x[:, half:]), fixed, keeps, e_ref, p_ref)
    p_bottom_ref[ENC_ROWS // 2 * 3 * maps :, :] = jnp.zeros(
        (p_bottom_ref.shape[0] - ENC_ROWS // 2 * 3 * maps, half), BF
    )
    few = ENC_ROWS // 2
    p3 = [(0, few, p_top_ref), (few, rows // 2, p3_ref), (rows // 2, rows // 2 + few + MID_ROWS, p_bottom_ref)]
    total = rows // 2 + 2
    first, stop = early_middle(rows)
    keeps = [keep_top] + [None] * (total - 2) + [keep_bottom]
    for g in range(-(-total // MID_ROWS)):
        start = g * MID_ROWS
        if g < first:
            narrow(mid_ref[...], p3, fixed, start, keeps[start : start + MID_ROWS], m_top_ref, start)
        elif g >= stop:
            narrow(
                mid_ref[...], p3, fixed, start, keeps[start : start + MID_ROWS], m_bottom_ref, start - stop * MID_ROWS
            )


def decode_kernel(
    x_ref, mask_ref, e_top_ref, e4_ref, e_bottom_ref, m_top_ref, m_ref, m_bottom_ref, dec_ref, wout_ref, bdec_ref, bout_ref,
    out_ref,
):
    rows, length = x_ref.shape
    half = length // 2
    span = bdec_ref.shape[0] * 2
    span_m = bdec_ref.shape[0] * 3
    total = rows // 2 + 2
    first, stop = early_middle(rows)
    e4 = [(0, ENC_ROWS, e_top_ref), (ENC_ROWS, rows, e4_ref), (rows, rows + EDGE, e_bottom_ref)]
    m3 = [
        (0, first * MID_ROWS, m_top_ref),
        (first * MID_ROWS, stop * MID_ROWS, m_ref),
        (stop * MID_ROWS, total, m_bottom_ref),
    ]
    alive = column(mask_ref[...].astype(F32), rows)
    bias = jnp.concatenate([bdec_ref[...]] * DEC_ROWS, axis=0)
    depth = half
    steps = dec_ref.shape[1] // depth
    units = OUT_ROWS // DEC_ROWS
    tiles = DEC_ROWS * bdec_ref.shape[0] * units // depth

    def finish(*accs):
        sums = [accs[:units], accs[units : 2 * units]]
        outs = accs[2 * units :]
        turn = [0] * units
        waiting = None

        def push(tile, unit):
            slot = turn[unit] % 2
            turn[unit] += 1
            pltpu.matmul_push_rhs(tile, slot, unit)
            return slot

        def project(item):
            top, decoded = item
            unit = top // OUT_ROWS % units
            for k in range(tiles):
                slot = push(decoded[k * depth : (k + 1) * depth], unit)
                pltpu.matmul_acc_lhs(outs[unit], wout_ref[:, k * depth : (k + 1) * depth], load_staged_rhs=slot)
            branch = pltpu.matmul_pop(outs[unit])
            for q in range(2):
                own = x_ref[top : top + OUT_ROWS, q * half : (q + 1) * half]
                value = own + branch[q * OUT_ROWS : (q + 1) * OUT_ROWS] + bout_ref[0]
                out_ref[top : top + OUT_ROWS, q * half : (q + 1) * half] = (
                    alive[top : top + OUT_ROWS] * value
                ).astype(BF)

        for top in range(0, rows, OUT_ROWS):
            windows = []
            for start in range(top, top + OUT_ROWS, DEC_ROWS):
                low = start + EDGE // 2 - 1
                windows.append(
                    jnp.concatenate(
                        rows_from(e4, low, low + DEC_ROWS + 2, span)
                        + rows_from(m3, start // 2, start // 2 + DEC_ROWS // 2 + 2, span_m),
                        axis=0,
                    )
                )
            now = sums[top // OUT_ROWS % 2]
            for k in range(steps):
                slots = [push(w[k * depth : (k + 1) * depth], unit) for unit, w in enumerate(windows)]
                for acc, slot in zip(now, slots):
                    pltpu.matmul_acc_lhs(acc, dec_ref[:, k * depth : (k + 1) * depth], load_staged_rhs=slot)
            if waiting:
                project(waiting)
            waiting = top, jnp.concatenate([relu(pltpu.matmul_pop(acc) + bias) for acc in now], axis=0)
        project(waiting)

    pl.run_scoped(
        finish,
        *(pltpu.ACC(unit)((dec_ref.shape[0], half), F32) for _ in range(2) for unit in range(units)),
        *(pltpu.ACC(unit)((wout_ref.shape[0], half), F32) for unit in range(units)),
    )


def products(spectra, ta_ref, tb_ref, tf_ref, put):
    tmpl, rows, length = ta_ref.shape
    count = len(spectra)
    for lane in range(0, length, 128):
        real = {}
        imag = {}
        for c in range(0, rows, 8):
            at = [ta_ref[r, c : c + 8, lane : lane + 128] for r in range(tmpl)]
            bt = [tb_ref[r, c : c + 8, lane : lane + 128] for r in range(tmpl)]
            af = at if lane else [tf_ref[r, c : c + 8, :] for r in range(tmpl)]
            for i in range(count):
                ax = spectra[i][c : c + 8, lane : lane + 128]
                bx = spectra[i][c : c + 8, length + lane : length + lane + 128]
                for r in range(tmpl):
                    re = ax * at[r] + bx * bt[r]
                    im = bx * af[r] - ax * bt[r]
                    real[r, i] = re if c == 0 else real[r, i] + re
                    imag[r, i] = im if c == 0 else imag[r, i] + im
        for r in range(tmpl):
            for i in range(count):
                put(r, i, lane, jnp.sum(real[r, i], axis=0, keepdims=True))
                put(r, i, length + lane, jnp.sum(imag[r, i], axis=0, keepdims=True))


def own_kernel(
    x_ref, t_ref, table_ref, split_ref, perm_ref, assign_ref,
    a_ref, b_ref, first_ref, p_ref, copy_ref, order_ref, s_ref, natural_ref, sems,
):
    fetch = pltpu.make_async_copy(assign_ref, order_ref, sems.at[0])
    fetch.start()
    natural_ref[...] = dot_nt(x_ref[...], perm_ref[...]).astype(BF)
    store = pltpu.make_async_copy(natural_ref, copy_ref, sems.at[1])
    store.start()
    tmpl, rows, length = t_ref.shape
    s_ref[...] = dot(x_ref[...], split_ref[...])
    fetch.wait()
    for r in range(tmpl):
        y = dot(t_ref[order_ref[r] % tmpl], table_ref[...])
        a = y[:, :length]
        b = y[:, length:]
        lane = iota((rows, 128), 1)
        a_ref[r] = a
        b_ref[r] = b
        b_ref[r, :, :128] = jnp.where(lane == 0, 0.0, b[:, :128])
        first_ref[r] = jnp.where(lane == 0, b[:, :128], a[:, :128])

    def put(r, i, lane, row):
        p_ref[r : r + 1, lane : lane + 128] = row

    products([s_ref], a_ref, b_ref, first_ref, put)
    store.wait()


def other_kernel(x_ref, ta_ref, tb_ref, tf_ref, split_ref, before_ref, p_ref, s_ref):
    del before_ref
    s_ref[...] = dot(x_ref[...], split_ref[...])

    def put(r, i, lane, row):
        p_ref[r : r + 1, lane : lane + 128] = row

    products([s_ref], ta_ref, tb_ref, tf_ref, put)


def corr_kernel(count, *refs):
    part_refs = refs[: count - 1]
    x_ref, ta_ref, tb_ref, tf_ref, table_ref, split_ref = refs[count - 1 : count + 5]
    keep_ref, send_ref, s_ref, p_ref, share_ref = refs[count + 5 :]
    tmpl, _, length = ta_ref.shape
    here = lax.axis_index("tmpl")
    for i, part_ref in enumerate(part_refs):
        p_ref[(here - i) % count] = part_ref[...]
    s_ref[...] = dot(x_ref[...], split_ref[...])

    def put(r, i, lane, row):
        p_ref[(here + 1) % count, r : r + 1, lane : lane + 128] = row

    products([s_ref], ta_ref, tb_ref, tf_ref, put)
    p = jnp.concatenate([p_ref[i, r : r + 1, :] for r in range(tmpl) for i in range(count)], axis=0)
    lane = iota(p.shape, 1)
    p = jnp.where((lane == 0) | (lane == length), p * 0.5, p)
    high = p.astype(BF)
    low = (p - high.astype(F32)).astype(BF)
    pairs = tmpl * count
    both = jnp.concatenate([high, low], axis=0)
    half = length // 2

    def part(first):
        y = sum(dot_nt(both[:, at : at + half], table_ref[:, at : at + half]) for at in (first, length + first))
        return (y[:pairs] + y[pairs:]) * (1.0 / length)

    even = part(0)
    uneven = part(half)
    near = even + uneven
    far = even - uneven
    block = iota(far.shape, 0) % count
    later = jnp.where(block == count - 1, 0.0, pltpu.roll(far, pairs - 1, 0))
    parity = lax.axis_index("tm")
    far = jnp.where(parity == 1, far, later)
    width = share_ref.shape[3]
    chans = share_ref.shape[1]
    for c in range(chans):
        share_ref[0, c] = near[:, c * width : (c + 1) * width]
        share_ref[1, c] = far[:, c * width : (c + 1) * width]
    chan = lax.axis_index("chan")
    mine = chan // 2 * 2 + parity
    for k in range(chans):
        to = mine ^ k
        kind = (to + parity) % 2
        keep_ref[k] = share_ref[kind, to // 2 * 2 + chan % 2]
        send_ref[k] = share_ref[kind, to // 2 * 2 + 1 - chan % 2].astype(BF)


def fold_kernel(keep_ref, got_ref, own_ref, *outs):
    own_ref[...] = keep_ref[0] + got_ref[0].astype(F32)
    for k, out in enumerate(outs):
        out[...] = (keep_ref[k + 1] + got_ref[k + 1].astype(F32)).astype(BF)


VMEM = pltpu.MemorySpace.VMEM
HBM = pltpu.MemorySpace.HBM
SMEM = pltpu.MemorySpace.SMEM


def call(kernel, outs, scratch=(), hbm=(), smem=(), hbm_out=(), inputs=0):
    def run(*args):
        return inner(*[pltpu.with_memory_space_constraint(x, HBM) if i in hbm else x for i, x in enumerate(args)])

    inner = pl.pallas_call(
        kernel,
        out_shape=tuple(jax.ShapeDtypeStruct(s, d) for s, d in outs),
        in_specs=[pl.BlockSpec(memory_space=HBM if i in hbm else SMEM if i in smem else VMEM) for i in range(inputs)],
        out_specs=tuple(pl.BlockSpec(memory_space=HBM if i in hbm_out else VMEM) for i in range(len(outs))),
        scratch_shapes=scratch,
        compiler_params=pltpu.CompilerParams(vmem_limit_bytes=48 * 1024 * 1024),
    )
    return run


def rotated(x, axes, by):
    count = lax.axis_size(axes)
    return lax.ppermute(x, axes, [(i, (i + by) % count) for i in range(count)])


def body(raw, dead_mask, templates, assign, w_enc, b_enc, w_mid, b_mid, w_dec, b_dec, w_out, b_out):
    rows, length = raw.shape
    half = length // 2
    maps = w_enc.shape[0]
    chans = lax.axis_size("chan")
    blocks = lax.axis_size("tmpl")
    tmpl = templates.shape[0]
    small = [
        raw,
        dead_mask[None],
        w_enc.transpose(1, 2, 3, 0),
        w_mid.transpose(2, 3, 1, 0),
        w_dec.transpose(2, 3, 0, 1),
        b_enc[None],
        b_mid[None],
        b_dec[None],
        w_out[None],
    ]
    *loaded, send1, send2, perm = call(
        load_kernel,
        [(x.shape, x.dtype) for x in small] + [((EDGE, length), BF)] * 2 + [((length, length), BF)],
        [pltpu.SemaphoreType.DMA((len(small),))],
        hbm=range(len(small)),
        inputs=len(small),
    )(*small)
    r1 = lax.ppermute(send1, "chan", [(i, i ^ 1) for i in range(chans) if i ^ 1 < chans])
    links = [(i, i + 1) for i in range(1, chans - 1, 2)]
    r2 = lax.ppermute(send2, "chan", links + [(b, a) for a, b in links])

    dec_cols = (DEC_ROWS + 2) * 4 * maps + (DEC_ROWS // 2 + 2) * 6 * maps
    enc_w, mid_w, dec_w, out_w, dec_b = call(
        prep_kernel,
        [
            ((ENC_ROWS * 2 * maps, 4 * (ENC_ROWS + EDGE) + PAD), BF),
            ((MID_ROWS * 2 * maps, (MID_ROWS + 2) * 3 * maps + PAD), BF),
            ((DEC_ROWS * 2 * maps, dec_cols), BF),
            ((2 * OUT_ROWS, OUT_ROWS * 2 * maps), BF),
            ((2 * maps, half), F32),
        ],
        [pltpu.VMEM((DEC_ROWS * 2 * maps, dec_cols), F32)],
        inputs=7,
    )(*loaded[2:9])
    first, stop = early_middle(rows)
    x, e4, p3, m3 = call(
        inner_kernel,
        [
            ((rows, length), F32),
            (((rows - ENC_ROWS) * 4 * maps, half), BF),
            (((rows - ENC_ROWS) // 2 * 3 * maps, half), BF),
            (((stop - first) * MID_ROWS * 6 * maps, half), BF),
        ],
        inputs=5,
    )(*loaded[:2], perm, enc_w, mid_w)
    e_top, e_bottom, m_top, m_bottom = call(
        edge_kernel,
        [
            ((ENC_ROWS * 4 * maps, half), BF),
            ((ENC_ROWS * 4 * maps, half), BF),
            ((first * MID_ROWS * 6 * maps, half), BF),
            (((rows // 2 + 2 - stop * MID_ROWS) * 6 * maps, half), BF),
        ],
        [
            pltpu.VMEM((ENC_ROWS // 2 * 3 * maps, half), BF),
            pltpu.VMEM(((ENC_ROWS // 2 + MID_ROWS) * 3 * maps, half), BF),
        ],
        inputs=7,
    )(x, perm, r1, r2, p3, enc_w, mid_w)
    (denoised,) = call(
        decode_kernel, [((rows, length), BF)], smem=(11,), inputs=12
    )(x, loaded[1], e_top, e4, e_bottom, m_top, m3, m_bottom, dec_w, out_w, dec_b, b_out)

    forward = jnp.asarray(forward_table(length))
    split = jnp.asarray(forward_table(length)[split_order(length)])
    gathered = []
    for k in range(1, blocks):
        gathered.append(rotated(denoised, "tmpl", k))
    *spectra, natural = call(
        own_kernel,
        [
            ((tmpl, rows, length), F32),
            ((tmpl, rows, length), F32),
            ((tmpl, rows, 128), F32),
            ((tmpl, 2 * length), F32),
            ((rows, length), BF),
        ],
        [
            pltpu.SMEM((tmpl,), jnp.int32),
            pltpu.VMEM((rows, 2 * length), F32),
            pltpu.VMEM((rows, length), BF),
            pltpu.SemaphoreType.DMA((2,)),
        ],
        hbm=(5,),
        hbm_out=(4,),
        inputs=6,
    )(denoised, templates, forward, split, perm, assign)
    width = length // chans
    pairs = tmpl * blocks
    sums = [spectra.pop()]
    for x in gathered[:-1]:
        (more,) = call(
            other_kernel, [((tmpl, 2 * length), F32)], [pltpu.VMEM((rows, 2 * length), F32)], inputs=6
        )(x, *spectra, split, sums[-1])
        sums.append(more)
    keep, send = call(
        functools.partial(corr_kernel, blocks),
        [((chans, pairs, width), F32), ((chans, pairs, width), BF)],
        [
            pltpu.VMEM((rows, 2 * length), F32),
            pltpu.VMEM((blocks, tmpl, 2 * length), F32),
            pltpu.VMEM((2, chans, pairs, width), F32),
        ],
        inputs=blocks + 5,
    )(*sums, gathered[-1], *spectra, forward, split)
    got = lax.ppermute(send, "chan", [(i, i ^ 1) for i in range(chans)])
    total, *parts = call(
        fold_kernel, [((pairs, width), F32)] + [((pairs, width), BF)] * (chans - 1), inputs=2
    )(keep, got)
    for k, part in enumerate(parts, 1):
        step = k // 2 * 4 + k % 2
        got = lax.ppermute(part, ("chan", "tm"), [(i, i ^ step) for i in range(2 * chans)])
        total = total + got.astype(F32)
    return natural, total.reshape(tmpl, blocks, 1, width)


def solution(mesh):
    return jax.shard_map(
        body,
        mesh=mesh,
        in_specs=(
            P("chan", ("tmpl", "tm")),
            P("chan"),
            P("tmpl", "chan", None),
            P("tmpl"),
            P(),
            P(),
            P(),
            P(),
            P(),
            P(),
            P(),
            P(),
        ),
        out_specs=(P("chan", ("tmpl", "tm")), P("tmpl", None, "tm", "chan")),
        check_vma=False,
    )
```

```python
import functools
import math

import jax
import jax.numpy as jnp
import numpy as np
from jax import lax
from jax.experimental import pallas as pl
from jax.experimental.pallas import tpu as pltpu
from jax.sharding import PartitionSpec as P


BF = jnp.bfloat16
F32 = jnp.float32
EDGE = 8
ENC_ROWS = 8
MID_ROWS = 3
DEC_ROWS = 4
OUT_ROWS = 8
PAD = 16


def frequency_order(patch_len):
    return np.concatenate([np.arange(0, patch_len, 2), np.arange(1, patch_len, 2)])


def forward_table(patch_len):
    s = np.arange(patch_len)[:, None]
    f = frequency_order(patch_len)[None, :]
    phase = ((s * f) % (2 * patch_len)).astype(np.float64) * (math.pi / patch_len)
    table = np.concatenate([np.cos(phase), np.sin(phase)], axis=1)
    table[:, patch_len] = 1.0 - 2.0 * (np.arange(patch_len) % 2)
    return table.astype(jnp.bfloat16)


def split_order(patch_len):
    return np.concatenate([np.arange(0, patch_len, 2), np.arange(1, patch_len, 2)])


def dot(a, b):
    return jnp.dot(a, b, preferred_element_type=F32)


def dot_nt(a, b):
    return lax.dot_general(a, b, (((1,), (1,)), ((), ())), preferred_element_type=F32)


def iota(shape, dim):
    return lax.broadcasted_iota(jnp.int32, shape, dim)


def column(row, count):
    m = row.shape[1]
    pick = iota((count, m), 0) % m == iota((count, m), 1)
    return jnp.sum(jnp.where(pick, row, 0.0), axis=1, keepdims=True)


def load_kernel(*refs):
    count = (len(refs) - 4) // 2
    sources = refs[:count]
    copies = refs[count : 2 * count]
    first_ref, second_ref, perm_ref, sems = refs[2 * count :]
    moves = [pltpu.make_async_copy(src, dst, sems.at[i]) for i, (src, dst) in enumerate(zip(sources, copies))]
    for move in moves:
        move.start()
    length = perm_ref.shape[0]
    half = length // 2
    s = iota((length, half), 0)
    t = iota((length, half), 1)
    perm_ref[:, :half] = jnp.where(s == 2 * t, 1.0, 0.0).astype(BF)
    perm_ref[:, half:] = jnp.where(s == 2 * t + 1, 1.0, 0.0).astype(BF)
    moves[0].wait()
    moves[1].wait()
    raw_ref, mask_ref = copies[:2]
    rows = raw_ref.shape[0]
    alive = column(mask_ref[...].astype(F32), rows)
    head = raw_ref[:EDGE].astype(F32) * alive[:EDGE]
    tail = raw_ref[rows - EDGE :].astype(F32) * alive[rows - EDGE :]
    odd = lax.axis_index("chan") % 2 == 1
    first_ref[...] = jnp.where(odd, head, tail).astype(BF)
    second_ref[...] = jnp.where(odd, tail, head).astype(BF)
    for move in moves[2:]:
        move.wait()


def thirds(x):
    high = x.astype(BF).astype(F32)
    middle = (x - high).astype(BF).astype(F32)
    return high, middle, x - high - middle


def prep_kernel(
    we_ref, wm_ref, wd_ref, be_ref, bm_ref, bd_ref, wo_ref, enc_ref, mid_ref, dec_ref, out_ref, bdec_ref, wide_ref
):
    maps = we_ref.shape[3]
    span = 2 * maps
    width = enc_ref.shape[1]
    window = ENC_ROWS + EDGE
    spread = jnp.where(iota((span, maps), 0) % maps == iota((span, maps), 1), 1.0, 0.0).astype(BF)
    we = jnp.concatenate([we_ref[0, y].astype(F32) for y in range(3)], axis=0).astype(BF)
    taps = dot_nt(spread, we)
    q = iota((span, width), 0) // maps
    col_id = iota((span, width), 1)
    dy = col_id % window - (EDGE // 2 - 1)
    dx = col_id // window - q
    tap = jnp.where((dy >= 0) & (dy < 3) & (dx >= 0) & (dx < 3), dy * 3 + dx, -1)
    band = jnp.zeros((span, width), F32)
    for t in range(9):
        band = jnp.where(tap == t, taps[:, t : t + 1], band)
    at = col_id - 4 * window
    fixed = jnp.zeros((span, width), F32)
    for t, part in enumerate(thirds(column(be_ref[...], span))):
        fixed = jnp.where(at == t, part, fixed)
    for r in range(ENC_ROWS):
        row = (pltpu.roll(band, r, 1) if r else band) + fixed
        enc_ref[r * span : (r + 1) * span, :] = row.astype(BF)
    rows, cols = mid_ref.shape
    wide_ref[:rows, :cols] = jnp.zeros((rows, cols), F32)
    wm = wm_ref[...].astype(F32).reshape(9 * maps, 2 * maps).T
    for r in range(MID_ROWS):
        wide_ref[r * 2 * maps : (r + 1) * 2 * maps, r * 3 * maps : r * 3 * maps + 9 * maps] = wm
    acc = wide_ref[:rows, :cols]
    at = iota((rows, cols), 1) - (cols - PAD)
    for t, part in enumerate(thirds(column(bm_ref[...], rows))):
        acc = jnp.where(at == t, part, acc)
    mid_ref[...] = acc.astype(BF)
    wide_ref[...] = jnp.zeros(wide_ref.shape, F32)
    skip_cols = (DEC_ROWS + 2) * 4 * maps
    k = [[wd_ref[y, x].astype(F32) for x in range(3)] for y in range(3)]
    ws = [jnp.concatenate([k[y][x][:, 2 * maps :] for x in range(3)], axis=1) for y in range(3)]
    split = ((0,), (1, 2)), ((0, 1), (2,))
    wu = {}
    for r in range(2):
        for q in range(2):
            for a in range(2):
                wu[r, q, a] = jnp.concatenate(
                    [sum(k[y][x][:, : 2 * maps] for y in split[r][a] for x in split[q][b]) for b in range(2)], axis=1
                )
    for r in range(DEC_ROWS):
        for q in range(2):
            top = (r * 2 + q) * maps
            for y in range(3):
                left = ((r + y) * 4 + q) * maps
                wide_ref[top : top + maps, left : left + 3 * maps] = ws[y]
            for a in range(2):
                left = skip_cols + ((r + 1) // 2 + a) * 6 * maps + q * 2 * maps
                wide_ref[top : top + maps, left : left + 4 * maps] = wu[r % 2, q, a]
    dec_ref[...] = wide_ref[...].astype(BF)
    n = out_ref.shape[1]
    repeat = jnp.where(iota((maps, n), 1) % maps == iota((maps, n), 0), 1.0, 0.0).astype(BF)
    weights = dot(wo_ref[...], repeat)
    r_id = iota(out_ref.shape, 0)
    c_id = iota(out_ref.shape, 1)
    same = (c_id // (2 * maps) == r_id % OUT_ROWS) & (c_id // maps % 2 == r_id // OUT_ROWS)
    out_ref[...] = jnp.where(same, weights, 0.0).astype(BF)
    bdec_ref[...] = jnp.broadcast_to(column(bd_ref[...], 2 * maps), bdec_ref.shape)


def shifted(x, by):
    width = x.shape[1]
    moved = pltpu.roll(x, (-by) % width, 1)
    cut = width // 2
    parts = [moved[:, :cut], moved[:, cut:]]
    at = 0 if by < 0 else 1
    edge = iota(parts[at].shape, 1) == (0 if by < 0 else width - cut - 1)
    parts[at] = jnp.where(edge, jnp.zeros((), x.dtype), parts[at])
    return jnp.concatenate(parts, axis=1)


def constants(half):
    return jnp.where(iota((PAD, half), 0) < 3, 1.0, 0.0).astype(BF)


def fourfold(even, uneven):
    return [shifted(uneven, -1), even, uneven, shifted(even, 1)]


def relu(y, keep=None):
    if keep is not None:
        y = y * keep
    return jnp.maximum(y.astype(BF), jnp.zeros((), BF))


def encode(weights, pieces, fixed, keeps, e4_ref, p3_ref):
    window = jnp.concatenate([jnp.concatenate(pieces, axis=0).astype(BF), fixed], axis=0)
    keep_encoded(dot(weights[:, : window.shape[0]], window), keeps, e4_ref, p3_ref)


def keep_encoded(y, keeps, e4_ref, p3_ref):
    span = y.shape[0] // ENC_ROWS
    maps = span // 2
    both = []
    for r in range(ENC_ROWS):
        piece = relu(y[r * span : (r + 1) * span], keeps[r])
        e4_ref[r * 2 * span : (r + 1) * 2 * span, :] = jnp.concatenate(fourfold(piece[:maps], piece[maps:]), axis=0)
        both.append(piece.astype(F32))
    for r in range(0, ENC_ROWS, 2):
        total = both[r] + both[r + 1]
        pooled = ((total[:maps] + total[maps:]) * 0.25).astype(BF)
        at = r // 2 * 3 * maps
        p3_ref[at : at + 3 * maps, :] = jnp.concatenate(
            [shifted(pooled, -1), pooled, shifted(pooled, 1)], axis=0
        )


def rows_from(parts, low, high, span):
    found = []
    for first, stop, ref in parts:
        a, b = max(low, first), min(high, stop)
        if a < b:
            found.append(ref[(a - first) * span : (b - first) * span, :])
    return found


def narrow(weights, parts, fixed, start, keeps, m3_ref, at):
    maps2 = weights.shape[0] // MID_ROWS
    window = rows_from(parts, start, start + MID_ROWS + 2, maps2 // 2 * 3)
    keep_middle(dot(weights, jnp.concatenate(window + [fixed], axis=0)), keeps, m3_ref, at)


def keep_middle(y, keeps, m3_ref, at):
    maps2 = y.shape[0] // MID_ROWS
    for r, keep in enumerate(keeps):
        piece = relu(y[r * maps2 : (r + 1) * maps2], keep)
        m3_ref[(at + r) * 3 * maps2 : (at + r + 1) * 3 * maps2, :] = jnp.concatenate(
            [shifted(piece, -1), piece, shifted(piece, 1)], axis=0
        )


def early_middle(rows):
    few = ENC_ROWS // 2
    first = -(-few // MID_ROWS)
    stop = (rows // 2 - MID_ROWS - 2) // MID_ROWS + 1
    return first, stop


def inner_kernel(raw_ref, mask_ref, perm_ref, enc_ref, mid_ref, x_ref, e4_ref, p3_ref, m3_ref):
    rows, length = raw_ref.shape
    half = length // 2
    alive = column(mask_ref[...].astype(F32), rows)
    x = dot((raw_ref[...].astype(F32) * alive).astype(BF), perm_ref[...])
    x_ref[...] = x
    four = fourfold(x[:, :half], x[:, half:])
    fixed = constants(half)
    maps = enc_ref.shape[0] // ENC_ROWS // 2
    span = 4 * maps
    pooled = 3 * maps * ENC_ROWS // 2
    for g in range(rows // ENC_ROWS - 1):
        top = g * ENC_ROWS
        encode(
            enc_ref[...],
            [piece[top : top + ENC_ROWS + EDGE] for piece in four],
            fixed,
            [None] * ENC_ROWS,
            e4_ref.at[top * span : (top + ENC_ROWS) * span],
            p3_ref.at[g * pooled : (g + 1) * pooled],
        )
    first, stop = early_middle(rows)
    parts = [(ENC_ROWS // 2, rows // 2, p3_ref)]
    for g in range(first, stop):
        narrow(mid_ref[...], parts, fixed, g * MID_ROWS, [None] * MID_ROWS, m3_ref, (g - first) * MID_ROWS)


def rest_kernel(
    x_ref, mask_ref, perm_ref, r1_ref, r2_ref, e4_ref, p3_ref, m_ref,
    enc_ref, mid_ref, dec_ref, wout_ref, bdec_ref, bout_ref,
    out_ref, e_top_ref, e_bottom_ref, p_top_ref, p_bottom_ref, m_top_ref, m_bottom_ref,
):
    rows, length = x_ref.shape
    half = length // 2
    maps2 = bdec_ref.shape[0]
    span = maps2 * 2
    span_m = maps2 * 3
    total = rows // 2 + 2
    first, stop = early_middle(rows)
    few = ENC_ROWS // 2
    here = lax.axis_index("chan")
    last = lax.axis_size("chan") - 1
    odd = here % 2 == 1
    keep_top = jnp.where(here == 0, 0.0, 1.0)
    keep_bottom = jnp.where(here == last, 0.0, 1.0)
    e4 = [(0, ENC_ROWS, e_top_ref), (ENC_ROWS, rows, e4_ref), (rows, rows + EDGE, e_bottom_ref)]
    p3 = [(0, few, p_top_ref), (few, rows // 2, p3_ref), (rows // 2, rows // 2 + few + MID_ROWS, p_bottom_ref)]
    m3 = [
        (0, first * MID_ROWS, m_top_ref),
        (first * MID_ROWS, stop * MID_ROWS, m_ref),
        (stop * MID_ROWS, total, m_bottom_ref),
    ]
    alive = column(mask_ref[...].astype(F32), rows)
    bias = jnp.concatenate([bdec_ref[...]] * DEC_ROWS, axis=0)
    fixed = constants(half)
    depth = half
    steps = dec_ref.shape[1] // depth
    units = OUT_ROWS // DEC_ROWS
    tiles = DEC_ROWS * maps2 * units // depth
    p_bottom_ref[few * 3 * maps2 // 2 :, :] = jnp.zeros((p_bottom_ref.shape[0] - few * 3 * maps2 // 2, half), BF)

    sides = range(first), range(stop, -(-total // MID_ROWS))

    def finish(*accs):
        sums = [accs[:units], accs[units : 2 * units]]
        outs = accs[2 * units : 3 * units]
        edges = accs[3 * units : 4 * units]
        mids = accs[4 * units : 4 * units + len(sides[0])], accs[4 * units + len(sides[0]) :]
        turn = [0] * units

        def push(tile, unit):
            slot = turn[unit] % 2
            turn[unit] += 1
            pltpu.matmul_push_rhs(tile, slot, unit)
            return slot

        def project(top, now):
            decoded = jnp.concatenate([relu(pltpu.matmul_pop(acc) + bias) for acc in now], axis=0)
            unit = top // OUT_ROWS % units
            for k in range(tiles):
                slot = push(decoded[k * depth : (k + 1) * depth], unit)
                pltpu.matmul_acc_lhs(outs[unit], wout_ref[:, k * depth : (k + 1) * depth], load_staged_rhs=slot)
            branch = pltpu.matmul_pop(outs[unit])
            for q in range(2):
                own = x_ref[top : top + OUT_ROWS, q * half : (q + 1) * half]
                value = own + branch[q * OUT_ROWS : (q + 1) * OUT_ROWS] + bout_ref[0]
                out_ref[top : top + OUT_ROWS, q * half : (q + 1) * half] = (
                    alive[top : top + OUT_ROWS] * value
                ).astype(BF)

        def decode(top, now):
            windows = []
            for start in range(top, top + OUT_ROWS, DEC_ROWS):
                low = start + EDGE // 2 - 1
                windows.append(
                    jnp.concatenate(
                        rows_from(e4, low, low + DEC_ROWS + 2, span)
                        + rows_from(m3, start // 2, start // 2 + DEC_ROWS // 2 + 2, span_m),
                        axis=0,
                    )
                )
            for k in range(steps):
                slots = [push(w[k * depth : (k + 1) * depth], unit) for unit, w in enumerate(windows)]
                for acc, slot in zip(now, slots):
                    pltpu.matmul_acc_lhs(acc, dec_ref[:, k * depth : (k + 1) * depth], load_staged_rhs=slot)

        def split():
            r1 = r1_ref[...].astype(F32)
            r2 = r2_ref[...].astype(F32)
            lhs = jnp.concatenate([jnp.where(odd, r1, r2), jnp.where(odd, r2, r1)], axis=0).astype(BF)
            for k in range(length // depth):
                for unit in range(2):
                    slot = push(perm_ref[k * depth : (k + 1) * depth, unit * half : (unit + 1) * half], unit)
                    pltpu.matmul_acc_lhs(outs[unit], lhs[:, k * depth : (k + 1) * depth], load_staged_rhs=slot)

        def encode_edges():
            even, uneven = (pltpu.matmul_pop(outs[unit]) for unit in range(2))
            for unit in range(2):
                pair = []
                for q, part in enumerate((even, uneven)):
                    lanes = slice(q * half, (q + 1) * half)
                    if unit == 0:
                        pair.append(jnp.concatenate([part[:EDGE], x_ref[:ENC_ROWS, lanes]], axis=0))
                    else:
                        pair.append(jnp.concatenate([x_ref[rows - ENC_ROWS :, lanes], part[EDGE:]], axis=0))
                window = [jnp.concatenate(fourfold(*pair), axis=0).astype(BF), fixed]
                blank = depth - sum(w.shape[0] for w in window)
                window = jnp.concatenate(window + [jnp.zeros((blank, half), BF)], axis=0)
                slot = push(window, unit)
                pltpu.matmul_acc_lhs(edges[unit], enc_ref[...], load_staged_rhs=slot)

        def middle_edges():
            margin = EDGE // 2
            free = [None] * (ENC_ROWS - margin)
            keep_encoded(pltpu.matmul_pop(edges[0]), [keep_top] * margin + free, e_top_ref, p_top_ref)
            keep_encoded(pltpu.matmul_pop(edges[1]), free + [keep_bottom] * margin, e_bottom_ref, p_bottom_ref)
            for unit, groups in enumerate(sides):
                for i, g in enumerate(groups):
                    window = rows_from(p3, g * MID_ROWS, (g + 1) * MID_ROWS + 2, maps2 // 2 * 3)
                    slot = push(jnp.concatenate(window + [fixed], axis=0), unit)
                    pltpu.matmul_acc_lhs(mids[unit][i], mid_ref[...], load_staged_rhs=slot)

        def finish_edges():
            keeps = [keep_top] + [None] * (total - 2) + [keep_bottom]
            for unit, groups in enumerate(sides):
                for i, g in enumerate(groups):
                    y = pltpu.matmul_pop(mids[unit][i])
                    start = g * MID_ROWS
                    keep_middle(
                        y,
                        keeps[start : start + MID_ROWS],
                        m_bottom_ref if unit else m_top_ref,
                        start - (stop * MID_ROWS if unit else 0),
                    )

        tops = list(range(0, rows, OUT_ROWS))
        inside = [
            t
            for t in tops
            if t + EDGE // 2 - 1 >= ENC_ROWS
            and t + OUT_ROWS + EDGE // 2 + 1 <= rows
            and t // 2 >= first * MID_ROWS
            and t // 2 + OUT_ROWS // 2 + 2 <= stop * MID_ROWS
        ]
        between = [split, encode_edges, middle_edges, finish_edges]
        waiting = None
        for turn_of, top in enumerate(inside + [t for t in tops if t not in inside]):
            now = sums[turn_of % 2]
            if top not in inside:
                while between:
                    between.pop(0)()
            if between:
                between.pop(0)()
            decode(top, now)
            if waiting:
                project(*waiting)
            waiting = top, now
        project(*waiting)

    pl.run_scoped(
        finish,
        *(pltpu.ACC(unit)((dec_ref.shape[0], half), F32) for _ in range(2) for unit in range(units)),
        *(pltpu.ACC(unit)((wout_ref.shape[0], half), F32) for unit in range(units)),
        *(pltpu.ACC(unit)((enc_ref.shape[0], half), F32) for unit in range(units)),
        *(pltpu.ACC(unit)((mid_ref.shape[0], half), F32) for unit in range(units) for _ in sides[unit]),
    )


def products(spectra, ta_ref, tb_ref, tf_ref, put):
    tmpl, rows, length = ta_ref.shape
    count = len(spectra)
    for lane in range(0, length, 128):
        real = {}
        imag = {}
        for c in range(0, rows, 8):
            at = [ta_ref[r, c : c + 8, lane : lane + 128] for r in range(tmpl)]
            bt = [tb_ref[r, c : c + 8, lane : lane + 128] for r in range(tmpl)]
            af = at if lane else [tf_ref[r, c : c + 8, :] for r in range(tmpl)]
            for i in range(count):
                ax = spectra[i][c : c + 8, lane : lane + 128]
                bx = spectra[i][c : c + 8, length + lane : length + lane + 128]
                for r in range(tmpl):
                    re = ax * at[r] + bx * bt[r]
                    im = bx * af[r] - ax * bt[r]
                    real[r, i] = re if c == 0 else real[r, i] + re
                    imag[r, i] = im if c == 0 else imag[r, i] + im
        for r in range(tmpl):
            for i in range(count):
                put(r, i, lane, jnp.sum(real[r, i], axis=0, keepdims=True))
                put(r, i, length + lane, jnp.sum(imag[r, i], axis=0, keepdims=True))


def own_kernel(
    x_ref, t_ref, table_ref, split_ref, perm_ref, assign_ref,
    a_ref, b_ref, first_ref, p_ref, copy_ref, order_ref, s_ref, natural_ref, sems,
):
    fetch = pltpu.make_async_copy(assign_ref, order_ref, sems.at[0])
    fetch.start()
    natural_ref[...] = dot_nt(x_ref[...], perm_ref[...]).astype(BF)
    store = pltpu.make_async_copy(natural_ref, copy_ref, sems.at[1])
    store.start()
    tmpl, rows, length = t_ref.shape
    s_ref[...] = dot(x_ref[...], split_ref[...])
    fetch.wait()
    for r in range(tmpl):
        y = dot(t_ref[order_ref[r] % tmpl], table_ref[...])
        a = y[:, :length]
        b = y[:, length:]
        lane = iota((rows, 128), 1)
        a_ref[r] = a
        b_ref[r] = b
        b_ref[r, :, :128] = jnp.where(lane == 0, 0.0, b[:, :128])
        first_ref[r] = jnp.where(lane == 0, b[:, :128], a[:, :128])

    def put(r, i, lane, row):
        p_ref[r : r + 1, lane : lane + 128] = row

    products([s_ref], a_ref, b_ref, first_ref, put)
    store.wait()


def other_kernel(x_ref, ta_ref, tb_ref, tf_ref, split_ref, before_ref, p_ref, s_ref):
    del before_ref
    s_ref[...] = dot(x_ref[...], split_ref[...])

    def put(r, i, lane, row):
        p_ref[r : r + 1, lane : lane + 128] = row

    products([s_ref], ta_ref, tb_ref, tf_ref, put)


def corr_kernel(count, *refs):
    part_refs = refs[: count - 1]
    x_ref, ta_ref, tb_ref, tf_ref, table_ref, split_ref = refs[count - 1 : count + 5]
    keep_ref, send_ref, s_ref, p_ref, share_ref = refs[count + 5 :]
    tmpl, _, length = ta_ref.shape
    here = lax.axis_index("tmpl")
    for i, part_ref in enumerate(part_refs):
        p_ref[(here - i) % count] = part_ref[...]
    s_ref[...] = dot(x_ref[...], split_ref[...])

    def put(r, i, lane, row):
        p_ref[(here + 1) % count, r : r + 1, lane : lane + 128] = row

    products([s_ref], ta_ref, tb_ref, tf_ref, put)
    p = jnp.concatenate([p_ref[i, r : r + 1, :] for r in range(tmpl) for i in range(count)], axis=0)
    lane = iota(p.shape, 1)
    p = jnp.where((lane == 0) | (lane == length), p * 0.5, p)
    high = p.astype(BF)
    low = (p - high.astype(F32)).astype(BF)
    pairs = tmpl * count
    both = jnp.concatenate([high, low], axis=0)
    half = length // 2

    def part(first):
        y = sum(dot_nt(both[:, at : at + half], table_ref[:, at : at + half]) for at in (first, length + first))
        return (y[:pairs] + y[pairs:]) * (1.0 / length)

    even = part(0)
    uneven = part(half)
    near = even + uneven
    far = even - uneven
    block = iota(far.shape, 0) % count
    later = jnp.where(block == count - 1, 0.0, pltpu.roll(far, pairs - 1, 0))
    parity = lax.axis_index("tm")
    far = jnp.where(parity == 1, far, later)
    width = share_ref.shape[3]
    chans = share_ref.shape[1]
    for c in range(chans):
        share_ref[0, c] = near[:, c * width : (c + 1) * width]
        share_ref[1, c] = far[:, c * width : (c + 1) * width]
    chan = lax.axis_index("chan")
    mine = chan // 2 * 2 + parity
    for k in range(chans):
        to = mine ^ k
        kind = (to + parity) % 2
        keep_ref[k] = share_ref[kind, to // 2 * 2 + chan % 2]
        send_ref[k] = share_ref[kind, to // 2 * 2 + 1 - chan % 2].astype(BF)


def fold_kernel(keep_ref, got_ref, own_ref, *outs):
    own_ref[...] = keep_ref[0] + got_ref[0].astype(F32)
    for k, out in enumerate(outs):
        out[...] = (keep_ref[k + 1] + got_ref[k + 1].astype(F32)).astype(BF)


VMEM = pltpu.MemorySpace.VMEM
HBM = pltpu.MemorySpace.HBM
SMEM = pltpu.MemorySpace.SMEM


def call(kernel, outs, scratch=(), hbm=(), smem=(), hbm_out=(), inputs=0):
    def run(*args):
        return inner(*[pltpu.with_memory_space_constraint(x, HBM) if i in hbm else x for i, x in enumerate(args)])

    inner = pl.pallas_call(
        kernel,
        out_shape=tuple(jax.ShapeDtypeStruct(s, d) for s, d in outs),
        in_specs=[pl.BlockSpec(memory_space=HBM if i in hbm else SMEM if i in smem else VMEM) for i in range(inputs)],
        out_specs=tuple(pl.BlockSpec(memory_space=HBM if i in hbm_out else VMEM) for i in range(len(outs))),
        scratch_shapes=scratch,
        compiler_params=pltpu.CompilerParams(vmem_limit_bytes=48 * 1024 * 1024),
    )
    return run


def rotated(x, axes, by):
    count = lax.axis_size(axes)
    return lax.ppermute(x, axes, [(i, (i + by) % count) for i in range(count)])


def body(raw, dead_mask, templates, assign, w_enc, b_enc, w_mid, b_mid, w_dec, b_dec, w_out, b_out):
    rows, length = raw.shape
    half = length // 2
    maps = w_enc.shape[0]
    chans = lax.axis_size("chan")
    blocks = lax.axis_size("tmpl")
    tmpl = templates.shape[0]
    small = [
        raw,
        dead_mask[None],
        w_enc.transpose(1, 2, 3, 0),
        w_mid.transpose(2, 3, 1, 0),
        w_dec.transpose(2, 3, 0, 1),
        b_enc[None],
        b_mid[None],
        b_dec[None],
        w_out[None],
    ]
    *loaded, send1, send2, perm = call(
        load_kernel,
        [(x.shape, x.dtype) for x in small] + [((EDGE, length), BF)] * 2 + [((length, length), BF)],
        [pltpu.SemaphoreType.DMA((len(small),))],
        hbm=range(len(small)),
        inputs=len(small),
    )(*small)
    r1 = lax.ppermute(send1, "chan", [(i, i ^ 1) for i in range(chans) if i ^ 1 < chans])
    links = [(i, i + 1) for i in range(1, chans - 1, 2)]
    r2 = lax.ppermute(send2, "chan", links + [(b, a) for a, b in links])

    dec_cols = (DEC_ROWS + 2) * 4 * maps + (DEC_ROWS // 2 + 2) * 6 * maps
    enc_w, mid_w, dec_w, out_w, dec_b = call(
        prep_kernel,
        [
            ((ENC_ROWS * 2 * maps, half), BF),
            ((MID_ROWS * 2 * maps, (MID_ROWS + 2) * 3 * maps + PAD), BF),
            ((DEC_ROWS * 2 * maps, dec_cols), BF),
            ((2 * OUT_ROWS, OUT_ROWS * 2 * maps), BF),
            ((2 * maps, half), F32),
        ],
        [pltpu.VMEM((DEC_ROWS * 2 * maps, dec_cols), F32)],
        inputs=7,
    )(*loaded[2:9])
    first, stop = early_middle(rows)
    x, e4, p3, m3 = call(
        inner_kernel,
        [
            ((rows, length), F32),
            (((rows - ENC_ROWS) * 4 * maps, half), BF),
            (((rows - ENC_ROWS) // 2 * 3 * maps, half), BF),
            (((stop - first) * MID_ROWS * 6 * maps, half), BF),
        ],
        inputs=5,
    )(*loaded[:2], perm, enc_w, mid_w)
    (denoised,) = call(
        rest_kernel,
        [((rows, length), BF)],
        [
            pltpu.VMEM((ENC_ROWS * 4 * maps, half), BF),
            pltpu.VMEM((ENC_ROWS * 4 * maps, half), BF),
            pltpu.VMEM((ENC_ROWS // 2 * 3 * maps, half), BF),
            pltpu.VMEM(((ENC_ROWS // 2 + MID_ROWS) * 3 * maps, half), BF),
            pltpu.VMEM((first * MID_ROWS * 6 * maps, half), BF),
            pltpu.VMEM(((rows // 2 + 2 - stop * MID_ROWS) * 6 * maps, half), BF),
        ],
        smem=(13,),
        inputs=14,
    )(x, loaded[1], perm, r1, r2, e4, p3, m3, enc_w, mid_w, dec_w, out_w, dec_b, b_out)

    forward = jnp.asarray(forward_table(length))
    split = jnp.asarray(forward_table(length)[split_order(length)])
    gathered = []
    for k in range(1, blocks):
        gathered.append(rotated(denoised, "tmpl", k))
    *spectra, natural = call(
        own_kernel,
        [
            ((tmpl, rows, length), F32),
            ((tmpl, rows, length), F32),
            ((tmpl, rows, 128), F32),
            ((tmpl, 2 * length), F32),
            ((rows, length), BF),
        ],
        [
            pltpu.SMEM((tmpl,), jnp.int32),
            pltpu.VMEM((rows, 2 * length), F32),
            pltpu.VMEM((rows, length), BF),
            pltpu.SemaphoreType.DMA((2,)),
        ],
        hbm=(5,),
        hbm_out=(4,),
        inputs=6,
    )(denoised, templates, forward, split, perm, assign)
    width = length // chans
    pairs = tmpl * blocks
    sums = [spectra.pop()]
    for x in gathered[:-1]:
        (more,) = call(
            other_kernel, [((tmpl, 2 * length), F32)], [pltpu.VMEM((rows, 2 * length), F32)], inputs=6
        )(x, *spectra, split, sums[-1])
        sums.append(more)
    keep, send = call(
        functools.partial(corr_kernel, blocks),
        [((chans, pairs, width), F32), ((chans, pairs, width), BF)],
        [
            pltpu.VMEM((rows, 2 * length), F32),
            pltpu.VMEM((blocks, tmpl, 2 * length), F32),
            pltpu.VMEM((2, chans, pairs, width), F32),
        ],
        inputs=blocks + 5,
    )(*sums, gathered[-1], *spectra, forward, split)
    got = lax.ppermute(send, "chan", [(i, i ^ 1) for i in range(chans)])
    total, *parts = call(
        fold_kernel, [((pairs, width), F32)] + [((pairs, width), BF)] * (chans - 1), inputs=2
    )(keep, got)
    for k, part in enumerate(parts, 1):
        step = k // 2 * 4 + k % 2
        got = lax.ppermute(part, ("chan", "tm"), [(i, i ^ step) for i in range(2 * chans)])
        total = total + got.astype(F32)
    return natural, total.reshape(tmpl, blocks, 1, width)


def solution(mesh):
    return jax.shard_map(
        body,
        mesh=mesh,
        in_specs=(
            P("chan", ("tmpl", "tm")),
            P("chan"),
            P("tmpl", "chan", None),
            P("tmpl"),
            P(),
            P(),
            P(),
            P(),
            P(),
            P(),
            P(),
            P(),
        ),
        out_specs=(P("chan", ("tmpl", "tm")), P("tmpl", None, "tm", "chan")),
        check_vma=False,
    )
```
